32 devices in a mesh: seq: 16 (over z, y, x), head: 2 (over core).
Axes of the slice: x: 2, y: 2, z: 4, core: 2. Of those that a mesh axis runs over, the one named last changes fastest.
Arguments:
- queries: bfloat16 [8192, 2048], P('seq', 'head'), may hold values from -37.123106012293746 to 37.123106012293746
- keys: bfloat16 [8192, 2048], P('seq', 'head'), may hold values from -6 to 6
- values: bfloat16 [8192, 2048], P('seq', 'head'), may hold values from -24 to 24
- rand_blocks: int32 [128, 16], P('seq', 'head'), may hold values from 0 to 127, as said below
- global_blocks: int32 [2], replicated, may hold values from 0 to 127
- out_weight: bfloat16 [2048, 4096], P(('head', 'seq')), may hold values from -0.125 to 0.125
Outputs:
- layer_out: bfloat16 [8192, 4096], P(('seq', 'head'))
The draws below stay inside these ranges and needn't reach their ends.
Inputs may be any that keep to these rules, and one draw needn't show every extreme that they name: `rand_blocks`: of the 8 x 8 entries of one device, at most 8 name blocks of one and the same index of seq (block id // 8), and some index of seq is named exactly 8 times by them.
All inputs are finite; a program needn't handle non-finite values.
Results may differ from the reference program's by a relative error of at most 0.013.
Values may be sent and summed in bfloat16 or wider, within the bound.
A program may use at most 128 MiB of HBM per device.

```python
import jax
import jax.numpy as jnp
from jax import lax

D = 4096
H = 16
DH = 128
BLK = 64
G = 2
QB_DEV = 8
HG = 8
NQB = 128
TOKENS = 8192
CAP = 8
N_SEQ = 16
N_HEAD = 2


def draw_queries(key, part):
    drawn = jax.random.truncated_normal(jax.random.fold_in(key, 1), -6.0, 6.0, (TOKENS, H * DH), jnp.float32)
    return drawn.astype(jnp.bfloat16)


def draw_keys(key, part):
    drawn = jax.random.truncated_normal(jax.random.fold_in(key, 2), -6.0, 6.0, (TOKENS, H * DH), jnp.float32)
    return drawn.astype(jnp.bfloat16)


def draw_rand_blocks(key, part):
    total = QB_DEV * HG

    def single(subkey):
        key_first, key_rest, key_order, key_local = jax.random.split(subkey, 4)
        first = jax.random.randint(key_first, (), 0, N_SEQ)
        rest = jax.random.permutation(key_rest, N_SEQ * CAP - CAP)[:total - CAP] + CAP
        slots = jnp.concatenate([jnp.arange(CAP, dtype=jnp.int32), rest.astype(jnp.int32)])
        owners = (slots // CAP + first) % N_SEQ
        owners = jax.random.permutation(key_order, owners)
        local = jax.random.randint(key_local, (total,), 0, QB_DEV)
        return (owners * QB_DEV + local).astype(jnp.int32)
    subkeys = jax.random.split(jax.random.fold_in(key, 11), N_SEQ * N_HEAD)
    ids = jax.vmap(single)(subkeys).reshape(N_SEQ, N_HEAD, QB_DEV, HG)
    return ids.transpose(0, 2, 1, 3).reshape(NQB, H)


def level_of(own_key, extent, shards, least, top_value):
    factor_of, own = 1.0, jax.random.fold_in(own_key, 6)
    for position, blocks in shards:
        heights = jnp.exp(jax.random.uniform(jax.random.fold_in(own, position), (blocks,), jnp.float32, least / len(shards), top_value / len(shards)))
        factor_of = factor_of * jnp.repeat(heights, extent[position] // blocks).reshape([-1 if axis == position else 1 for axis in range(len(extent))])
    return factor_of


def normal_values(key, shape, scale, limit, cuts=(), kind=jnp.bfloat16):
    values = jax.random.normal(key, shape, jnp.float32) * scale
    if len(cuts) > 0:
        values = level_of(key, shape, cuts, -0.22, 0.18) * values
    return jnp.clip(values, min=-limit, max=limit).astype(kind)


def setup_inputs(seed: int = 0) -> dict:
    splits = jax.random.split(jax.random.key(seed), 7)
    return {
        "queries": draw_queries(jax.random.fold_in(splits[6], 71), 0),
        "keys": draw_keys(jax.random.fold_in(splits[6], 71), 0),
        "values": normal_values(splits[2], (TOKENS, H * DH), 4.0, 24.0, ((0, 16), (1, 2))),
        "rand_blocks": draw_rand_blocks(jax.random.fold_in(splits[6], 71), 0),
        "global_blocks": jax.random.randint(splits[4], (G,), 0, NQB).astype(jnp.int32),
        "out_weight": normal_values(splits[5], (H * DH, D), (H * DH) ** -0.5, 0.125, ((0, 32),)),
    }


def reference(queries, keys, values, rand_blocks, global_blocks, out_weight):
    f32 = jnp.float32
    query_blocks = queries.reshape(NQB, BLK, H, DH)
    key_blocks = keys.reshape(NQB, BLK, H, DH)
    value_blocks = values.reshape(NQB, BLK, H, DH)
    key_padded = jnp.concatenate([key_blocks[-1:], key_blocks, key_blocks[:1]], axis=0)
    value_padded = jnp.concatenate([value_blocks[-1:], value_blocks, value_blocks[:1]], axis=0)
    global_keys = key_blocks[global_blocks].reshape(G * BLK, H, DH).astype(f32)
    global_values = value_blocks[global_blocks].reshape(G * BLK, H, DH).astype(f32)
    head_iota = jnp.arange(H, dtype=jnp.int32)[None, :]
    group_width = H * DH // N_HEAD
    scale = DH ** -0.5

    def window_of(padded, start):
        beside_all = lax.dynamic_slice_in_dim(padded, start, QB_DEV + 2, 0)
        return jnp.concatenate([beside_all[:-2], beside_all[1:-1], beside_all[2:]], axis=1).astype(f32)

    def span(index):
        start = (index * QB_DEV).astype(jnp.int32)
        query_part = lax.dynamic_slice_in_dim(query_blocks, start, QB_DEV, 0).astype(f32)
        window_keys = window_of(key_padded, start)
        window_values = window_of(value_padded, start)
        chosen_ids = lax.dynamic_slice_in_dim(rand_blocks, start, QB_DEV, 0)
        random_keys = key_blocks[chosen_ids, :, head_iota, :].astype(f32)
        random_values = value_blocks[chosen_ids, :, head_iota, :].astype(f32)
        s_window = jnp.einsum("qbhd,qkhd->qhbk", query_part, window_keys)
        s_global = jnp.einsum("qbhd,khd->qhbk", query_part, global_keys)
        s_random = jnp.einsum("qbhd,qhkd->qhbk", query_part, random_keys)
        scores = jnp.concatenate([s_window, s_global, s_random], axis=-1) * scale
        top = jnp.max(scores, axis=-1, keepdims=True)
        expo = jnp.exp(scores - top)
        weights = (expo / jnp.sum(expo, axis=-1, keepdims=True)).astype(jnp.bfloat16).astype(f32)
        wlen = 3 * BLK
        glen = G * BLK
        context = jnp.einsum("qhbk,qkhd->qbhd", weights[..., :wlen], window_values)
        context = context + jnp.einsum("qhbk,khd->qbhd", weights[..., wlen:wlen + glen], global_values)
        context = context + jnp.einsum("qhbk,qhkd->qbhd", weights[..., wlen + glen:], random_values)
        attended = context.reshape(QB_DEV * BLK, H * DH).astype(jnp.bfloat16)
        summed = jnp.zeros((QB_DEV * BLK, D), f32)
        for group in range(N_HEAD):
            part = jnp.dot(attended[:, group * group_width:(group + 1) * group_width],
                           out_weight[group * group_width:(group + 1) * group_width],
                           preferred_element_type=f32).astype(jnp.bfloat16)
            part = lax.optimization_barrier(part)
            summed = summed + part.astype(f32)
        return summed.astype(jnp.bfloat16)

    result = lax.map(span, jnp.arange(N_SEQ, dtype=jnp.int32))
    return result.reshape(TOKENS, D)
```

```python
import functools

import jax
import jax.numpy as jnp
from jax import lax
from jax.experimental import pallas as pl
from jax.experimental.pallas import tpu as pltpu
from jax.sharding import PartitionSpec as P

MESH = pl.DeviceIdType.MESH
LANES = 128
TILE = 16


def ranked(owners):
    count = owners.shape[0]
    order = jnp.arange(count, dtype=jnp.int32)
    earlier = (owners[:, None] == owners[None, :]) & (order[None, :] < order[:, None])
    return jnp.sum(earlier.astype(jnp.int32), axis=1)


def layer_kernel(
    n, cap, blocks, block_len, head_dim, heads, scale,
    glob_ref, slot_ref, codes_ref, q_ref, k_ref, v_ref, w_ref,
    full_ref, o_ref,
    pairs, stage, arr, codes_in, codes, low, high, pair_x, send_x, pair_y, send_y, cut_z, got_z, shared,
    acc, top_s, sum_s,
    line_send, line_recv, near_send, near_recv, far_send, far_recv,
    code_send, code_recv, rand_send, rand_recv, edge_send, edge_recv,
    glob_send, glob_recv, zcut_send, zcut_recv, zgive_send, zgive_recv, local,
):
    lines = n // 4
    me = lax.axis_index("seq")
    z, y, x = me // 4, me // 2 % 2, me % 2
    other_y = z * 4 + (1 - y) * 2 + x
    other_x = z * 4 + y * 2 + 1 - x
    half = w_ref.shape[1] // 2
    tiles = block_len // TILE
    share = heads * tiles // lines
    wide = 2 * head_dim

    barrier = pltpu.get_barrier_semaphore()

    def greet(k, c):
        pl.semaphore_signal(
            barrier, inc=1, device_id={"seq": lax.rem(me + k, n)}, device_id_type=MESH
        )
        return c

    lax.fori_loop(1, n, greet, 0)
    pl.semaphore_wait(barrier, n - 1)

    def remote(src, dst, send, recv, target):
        return pltpu.make_async_remote_copy(
            src_ref=src, dst_ref=dst, send_sem=send, recv_sem=recv,
            device_id={"seq": target}, device_id_type=MESH,
        )

    def origin(side, t):
        return (z - t if side == 0 else z + t) * 4

    def exists(side, t):
        return z - t >= 0 if side == 0 else z + t < lines

    def held(side, t):
        return w_ref if t == 0 else full_ref.at[origin(side, t) + y * 2 + x]

    def along(side, t):
        target = me + 4 if side == 0 else me - 4
        index = origin(side, t) + y * 2 + x
        return remote(
            held(side, t), full_ref.at[index], line_send.at[side, t], line_recv.at[side, t], target
        )

    def passes(side, t):
        ahead = z + 1 < lines if side == 0 else z >= 1
        return jnp.logical_and(exists(side, t), ahead)

    def near(side, t, way):
        index = origin(side, t) + y * 2 + x
        return remote(
            held(side, t), full_ref.at[index], near_send.at[side, t, way],
            near_recv.at[side, t, way], other_y if way == 0 else other_x,
        )

    def far(side, t, way):
        index = origin(side, t) + (
            (1 - y) * 2 + x if way == 0 else y * 2 + 1 - x
        )
        cols = pl.ds(way * half, half)
        return remote(
            full_ref.at[index, :, cols], full_ref.at[index, :, cols], far_send.at[side, t, way],
            far_recv.at[side, t, way], other_x if way == 0 else other_y,
        )

    def sides(t):
        return (0,) if t == 0 else (0, 1)

    def advance(t):
        for side in (0, 1):
            if t > 0:
                @pl.when(exists(side, t))
                def _():
                    along(side, t - 1).wait_recv()
            if t < lines - 1:
                @pl.when(passes(side, t))
                def _():
                    along(side, t).start()
        for side in sides(t):
            @pl.when(exists(side, t))
            def _():
                near(side, t, 0).start()
                near(side, t, 1).start()

    def forward(t):
        for side in sides(t):
            @pl.when(exists(side, t))
            def _():
                for way in (0, 1):
                    near(side, t, way).wait_recv()
                    far(side, t, way).start()

    def code(k):
        target = lax.rem(me + k, n)
        return remote(
            codes_ref.at[target], codes_in.at[me], code_send.at[k], code_recv.at[k], target
        )

    def rand(k):
        target = lax.rem(me + k, n)
        return remote(
            stage.at[pl.ds(target * cap, cap)], arr.at[pl.ds(me * cap, cap)],
            rand_send.at[k], rand_recv.at[k], target,
        )

    def each(body):
        def step(k, c):
            body(k)
            return c
        lax.fori_loop(1, n, step, 0)

    each(lambda k: code(k).start())
    codes_in[pl.ds(me, 1)] = codes_ref[pl.ds(me, 1)]

    own_rows = pltpu.make_async_copy(w_ref, full_ref.at[me], local.at[0])
    own_rows.start()
    advance(0)

    tail = (blocks - 1) * block_len
    up, down = lax.rem(me + 1, n), lax.rem(me + n - 1, n)
    edges = []
    for i, ref in enumerate((k_ref, v_ref)):
        edges.append(remote(
            ref.at[tail : tail + block_len], low.at[i], edge_send.at[0, i], edge_recv.at[0, i], up
        ))
        edges.append(remote(
            ref.at[0:block_len], high.at[i], edge_send.at[1, i], edge_recv.at[1, i], down
        ))
    for copy in edges:
        copy.start()

    for b in range(blocks):
        rows = slice(b * block_len, (b + 1) * block_len)
        for h in range(heads):
            cols = slice(h * head_dim, (h + 1) * head_dim)
            pairs[b * heads + h, :, 0:head_dim] = k_ref[rows, cols]
            pairs[b * heads + h, :, head_dim:wide] = v_ref[rows, cols]

    def candidate(block, out, lead):
        for h in range(heads):
            pair = pairs[block % blocks * heads + h]
            for r in range(tiles):
                rows = slice(r * TILE, (r + 1) * TILE)
                out[(*lead, 0, h * tiles + r)] = pair[rows, 0:head_dim]
                out[(*lead, 1, h * tiles + r)] = pair[rows, head_dim:wide]

    away = glob_ref[1 - x]
    candidate(away, send_x, ())
    glob_x = remote(send_x, pair_x.at[1], glob_send.at[0], glob_recv.at[0], other_x)
    glob_x.start()
    mine = glob_ref[x]
    candidate(mine, pair_x, (0,))
    holder = mine // blocks
    pick_x = lax.rem(holder + x, 2)
    pick_y = lax.rem(holder // 2 + y, 2)
    pick_z = holder // 4

    each(lambda k: code(k).wait_recv())
    to_smem = pltpu.make_async_copy(codes_in, codes, local.at[1])
    to_smem.start()
    to_smem.wait()

    def pack(target, out, place):
        for s in range(cap):
            out[place * cap + s] = pairs[codes[target, 0, s]]

    def ship(k):
        target = lax.rem(me + k, n)
        pack(target, stage, target)
        rand(k).start()

    each(ship)
    pack(me, arr, me)

    glob_x.wait_recv()
    picked = pair_x.at[:, 1 - y]
    send_y[...] = picked[pick_x]
    glob_y = remote(send_y, pair_y.at[1], glob_send.at[1], glob_recv.at[1], other_y)
    glob_y.start()
    picked = pair_x.at[:, y]
    pair_y[0] = picked[pick_x]

    advance(1)

    def line(dz):
        return lax.rem(z + dz, lines)

    def zcut(dz):
        to = line(dz)
        return remote(
            cut_z.at[pl.ds(to * share, share)], got_z.at[z], zcut_send.at[dz], zcut_recv.at[dz],
            to * 4 + y * 2 + x,
        )

    def zgive(dz):
        piece = shared.at[x, y, pl.ds(z * share, share)]
        return remote(
            piece, piece, zgive_send.at[dz], zgive_recv.at[dz], line(dz) * 4 + y * 2 + x
        )

    glob_y.wait_recv()
    cut_z[...] = pair_y[pick_y]
    for dz in range(1, lines):
        zcut(dz).start()
    got_z[z] = cut_z[pl.ds(z * share, share)]

    forward(0)

    for dz in range(1, lines):
        zcut(dz).wait_recv()
    shared[x, y, pl.ds(z * share, share)] = got_z[pick_z]
    for dz in range(1, lines):
        zgive(dz).start()
    for dz in range(1, lines):
        zgive(dz).wait_recv()
    give_y = remote(
        shared.at[x, y], shared.at[x, y], glob_send.at[2], glob_recv.at[2], other_y
    )
    give_y.start()
    give_y.wait_recv()
    give_x = remote(shared.at[x], shared.at[x], glob_send.at[3], glob_recv.at[3], other_x)
    give_x.start()

    if lines > 2:
        advance(2)
    give_x.wait_recv()
    for copy in edges:
        copy.wait_recv()

    def begin(h, c):
        cols = pl.ds(pl.multiple_of(h * head_dim, head_dim), head_dim)
        kk = jnp.concatenate([low[0, :, cols], k_ref[:, cols], high[0, :, cols]], axis=0)
        vv = jnp.concatenate([low[1, :, cols], v_ref[:, cols], high[1, :, cols]], axis=0)
        chunk = pl.ds(h * tiles, tiles)
        kg = [shared[i, 0, chunk].reshape(block_len, head_dim) for i in range(2)]
        vg = [shared[i, 1, chunk].reshape(block_len, head_dim) for i in range(2)]
        for b in range(blocks):
            lo, hi = b * block_len, (b + 3) * block_len
            ks = jnp.concatenate([kk[lo:hi], *kg], axis=0)
            vs = jnp.concatenate([vv[lo:hi], *vg], axis=0)
            s = lax.dot_general(
                q_ref[lo : lo + block_len, cols], ks, (((1,), (1,)), ((), ())),
                preferred_element_type=jnp.float32,
            ) * scale
            top = jnp.max(s, axis=-1, keepdims=True)
            expo = jnp.exp(s - top)
            total = jnp.sum(expo, axis=-1, keepdims=True)
            rows = pl.ds(lo, block_len)
            acc[rows, cols] = jnp.dot(
                expo.astype(jnp.bfloat16), vs, preferred_element_type=jnp.float32
            )
            top_s[h, rows] = jnp.broadcast_to(top, (block_len, LANES))
            sum_s[h, rows] = jnp.broadcast_to(total, (block_len, LANES))
        return c

    def finish(h, c):
        cols = pl.ds(pl.multiple_of(h * head_dim, head_dim), head_dim)
        for b in range(blocks):
            e = b * heads + h
            pair = arr[slot_ref[e]]
            kr, vr = pair[:, 0:head_dim], pair[:, head_dim:wide]
            rows = pl.ds(b * block_len, block_len)
            s = lax.dot_general(
                q_ref[rows, cols], kr, (((1,), (1,)), ((), ())),
                preferred_element_type=jnp.float32,
            ) * scale
            before = top_s[h, rows, 0:1]
            top = jnp.maximum(before, jnp.max(s, axis=-1, keepdims=True))
            fade = jnp.exp(before - top)
            expo = jnp.exp(s - top)
            total = sum_s[h, rows, 0:1] * fade + jnp.sum(expo, axis=-1, keepdims=True)
            o = acc[rows, cols] * fade + jnp.dot(
                expo.astype(jnp.bfloat16), vr, preferred_element_type=jnp.float32
            )
            o_ref[rows, cols] = (o * (1.0 / total)).astype(o_ref.dtype)
        return c

    steps = [functools.partial(forward, 1)]
    for t in range(3, lines):
        steps += [functools.partial(advance, t), functools.partial(forward, t - 1)]
    cutoffs = [heads * i // len(steps) for i in range(len(steps) + 1)]
    for step, h0, h1 in zip(steps, cutoffs, cutoffs[1:]):
        if h1 > h0:
            lax.fori_loop(h0, h1, begin, 0)
        step()
    forward(lines - 1)

    each(lambda k: rand(k).wait_recv())
    lax.fori_loop(0, heads, finish, 0)

    for t in range(lines):
        for side in (0, 1):
            if t < lines - 1:
                @pl.when(passes(side, t))
                def _():
                    along(side, t).wait_send()
        for side in sides(t):
            @pl.when(exists(side, t))
            def _():
                for way in (0, 1):
                    near(side, t, way).wait_send()
                    far(side, t, way).wait()
    each(lambda k: code(k).wait_send())
    each(lambda k: rand(k).wait_send())
    for dz in range(1, lines):
        zcut(dz).wait_send()
        zgive(dz).wait_send()
    for copy in (glob_x, glob_y, give_y, give_x, *edges):
        copy.wait_send()
    own_rows.wait()


def layer(glob, places, codes, q, k, v, weight, n, cap, blocks, block_len, head_dim, heads):
    lines = n // 4
    rows, columns = weight.shape
    tokens, width = q.shape
    tiles = heads * block_len // TILE
    dma = pltpu.SemaphoreType.DMA
    vmem = pl.BlockSpec(memory_space=pltpu.VMEM)
    smem = pl.BlockSpec(memory_space=pltpu.SMEM)
    hbm = pl.BlockSpec(memory_space=pl.ANY)
    kind = q.dtype
    f32 = jnp.float32
    slots = (n * cap, block_len, 2 * head_dim)
    tile = (TILE, LANES)
    return pl.pallas_call(
        functools.partial(
            layer_kernel, n, cap, blocks, block_len, head_dim, heads, head_dim ** (-0.5)
        ),
        out_shape=(
            jax.ShapeDtypeStruct((n, rows, columns), kind),
            jax.ShapeDtypeStruct((tokens, width), kind),
        ),
        in_specs=[smem, smem, vmem, vmem, vmem, vmem, vmem],
        out_specs=(hbm, vmem),
        scratch_shapes=[
            pltpu.VMEM((blocks * heads, block_len, 2 * head_dim), kind),
            pltpu.VMEM(slots, kind),
            pltpu.VMEM(slots, kind),
            pltpu.VMEM(codes.shape, jnp.int32),
            pltpu.SMEM(codes.shape, jnp.int32),
            pltpu.VMEM((2, block_len, width), kind),
            pltpu.VMEM((2, block_len, width), kind),
            pltpu.VMEM((2, 2, tiles, *tile), kind),
            pltpu.VMEM((2, tiles, *tile), kind),
            pltpu.VMEM((2, tiles, *tile), kind),
            pltpu.VMEM((tiles, *tile), kind),
            pltpu.VMEM((tiles, *tile), kind),
            pltpu.VMEM((lines, tiles // lines, *tile), kind),
            pltpu.VMEM((2, 2, tiles, *tile), kind),
            pltpu.VMEM((tokens, width), f32),
            pltpu.VMEM((heads, tokens, LANES), f32),
            pltpu.VMEM((heads, tokens, LANES), f32),
            dma((2, lines)), dma((2, lines)),
            dma((2, lines, 2)), dma((2, lines, 2)),
            dma((2, lines, 2)), dma((2, lines, 2)),
            dma((n,)), dma((n,)), dma((n,)), dma((n,)),
            dma((2, 2)), dma((2, 2)),
            dma((4,)), dma((4,)),
            dma((lines,)), dma((lines,)), dma((lines,)), dma((lines,)),
            dma((2,)),
        ],
        compiler_params=pltpu.CompilerParams(
            collective_id=0, has_side_effects=True, vmem_limit_bytes=48 << 20
        ),
        cost_estimate=pl.CostEstimate(
            flops=4 * tokens * 6 * block_len * width,
            transcendentals=tokens * 6 * block_len * heads,
            bytes_accessed=40 * n * rows * columns,
        ),
        name="layer",
    )(glob, places, codes, q, k, v, weight)


def body(queries, keys, values, rand_blocks, global_blocks, out_weight):
    f32 = jnp.float32
    n = lax.axis_size("seq")
    block_count, head_count = rand_blocks.shape
    tokens, width = queries.shape
    block_len = tokens // block_count
    head_dim = width // head_count
    entries = block_count * head_count
    cap = max(2, (2 * entries + n - 1) // n)

    flat_blocks = rand_blocks.reshape(entries)
    owners = flat_blocks // block_count
    head_iota = jnp.arange(entries, dtype=jnp.int32) % head_count
    codes = flat_blocks % block_count * head_count + head_iota
    ranks = ranked(owners)
    target = jnp.arange(n, dtype=jnp.int32)[:, None, None]
    slot = jnp.arange(LANES, dtype=jnp.int32)[None, :, None]
    hits = (owners[None, None, :] == target) & (ranks[None, None, :] == slot)
    outgoing = jnp.sum(jnp.where(hits, codes[None, None, :], 0), axis=2)

    group_rows, attended = layer(
        global_blocks, owners * cap + ranks, outgoing.reshape(n, 1, LANES), queries, keys, values,
        out_weight, n, cap, block_count, block_len, head_dim, head_count,
    )
    group_rows = group_rows.reshape(n * out_weight.shape[0], out_weight.shape[1])
    partial_value = jnp.dot(attended, group_rows, preferred_element_type=f32)
    return lax.psum_scatter(
        partial_value.astype(jnp.bfloat16), "head", scatter_dimension=0, tiled=True
    )


def solution(mesh):
    placed = (
        P("seq", "head"),
        P("seq", "head"),
        P("seq", "head"),
        P("seq", "head"),
        P(),
        P(("head", "seq"), None),
    )
    return jax.shard_map(
        body, mesh=mesh, in_specs=placed, out_specs=P(("seq", "head"), None), check_vma=False
    )
```

```python
import functools

import jax
import jax.numpy as jnp
from jax import lax
from jax.experimental import pallas as pl
from jax.experimental.pallas import tpu as pltpu
from jax.sharding import PartitionSpec as P

MESH = pl.DeviceIdType.MESH
LANES = 128


def ranked(owners):
    count = owners.shape[0]
    order = jnp.arange(count, dtype=jnp.int32)
    earlier = (owners[:, None] == owners[None, :]) & (order[None, :] < order[:, None])
    return jnp.sum(earlier.astype(jnp.int32), axis=1)


def layer_kernel(
    n, cap, blocks, block_len, head_dim, heads, scale,
    glob_ref, slot_ref, codes_ref, q_hbm, k_hbm, v_hbm, w_ref,
    out_ref,
    q_ref, k_ref, v_ref, full_ref, att, give, take,
    pairs, stage, arr, codes_in, codes, low, high, cand, got_p, got_z, shared,
    acc, top_s, sum_s,
    line_send, line_recv, near_send, near_recv, far_send, far_recv,
    code_send, code_recv, rand_send, rand_recv, edge_send, edge_recv,
    cut_send, cut_recv, line_out, line_in, give_send, give_recv, core_send, core_recv, local,
):
    lines = n // 4
    me = lax.axis_index("seq")
    z, y, x = me // 4, me // 2 % 2, me % 2
    other_y = z * 4 + (1 - y) * 2 + x
    other_x = z * 4 + y * 2 + 1 - x
    half = w_ref.shape[1] // 2
    part = heads // 2
    wide = 2 * head_dim

    hd = lax.axis_index("head")
    loads = [
        pltpu.make_async_copy(src, dst, local.at[2 + i])
        for i, (src, dst) in enumerate(((k_hbm, k_ref), (v_hbm, v_ref), (q_hbm, q_ref)))
    ]
    for copy in loads:
        copy.start()

    barrier = pltpu.get_barrier_semaphore()

    def greet(k, c):
        pl.semaphore_signal(
            barrier, inc=1, device_id={"seq": lax.rem(me + k, n)}, device_id_type=MESH
        )
        return c

    lax.fori_loop(1, n, greet, 0)
    pl.semaphore_signal(barrier, inc=1, device_id={"head": 1 - hd}, device_id_type=MESH)
    pl.semaphore_wait(barrier, n)

    def remote(src, dst, send, recv, target):
        return pltpu.make_async_remote_copy(
            src_ref=src, dst_ref=dst, send_sem=send, recv_sem=recv,
            device_id={"seq": target}, device_id_type=MESH,
        )

    def origin(side, t):
        return (z - t if side == 0 else z + t) * 4

    def exists(side, t):
        return z - t >= 0 if side == 0 else z + t < lines

    def held(side, t):
        return w_ref if t == 0 else full_ref.at[origin(side, t) + y * 2 + x]

    def along(side, t):
        target = me + 4 if side == 0 else me - 4
        index = origin(side, t) + y * 2 + x
        return remote(
            held(side, t), full_ref.at[index], line_send.at[side, t], line_recv.at[side, t], target
        )

    def passes(side, t):
        ahead = z + 1 < lines if side == 0 else z >= 1
        return jnp.logical_and(exists(side, t), ahead)

    def near(side, t, way):
        index = origin(side, t) + y * 2 + x
        return remote(
            held(side, t), full_ref.at[index], near_send.at[side, t, way],
            near_recv.at[side, t, way], other_y if way == 0 else other_x,
        )

    def far(side, t, way):
        index = origin(side, t) + (
            (1 - y) * 2 + x if way == 0 else y * 2 + 1 - x
        )
        cols = pl.ds(way * half, half)
        return remote(
            full_ref.at[index, :, cols], full_ref.at[index, :, cols], far_send.at[side, t, way],
            far_recv.at[side, t, way], other_x if way == 0 else other_y,
        )

    def sides(t):
        return (0,) if t == 0 else (0, 1)

    def advance(t):
        for side in (0, 1):
            if t > 0:
                @pl.when(exists(side, t))
                def _():
                    along(side, t - 1).wait_recv()
            if t < lines - 1:
                @pl.when(passes(side, t))
                def _():
                    along(side, t).start()
        for side in sides(t):
            @pl.when(exists(side, t))
            def _():
                near(side, t, 0).start()
                near(side, t, 1).start()

    def forward(t):
        for side in sides(t):
            @pl.when(exists(side, t))
            def _():
                for way in (0, 1):
                    near(side, t, way).wait_recv()
                    far(side, t, way).start()

    def code(k):
        target = lax.rem(me + k, n)
        return remote(
            codes_ref.at[target], codes_in.at[me], code_send.at[k], code_recv.at[k], target
        )

    def stride(k):
        return lax.rem(me + lax.rem(k * (n // 2 - 1), n), n)

    def rand(k):
        target = stride(k)
        return remote(
            stage.at[pl.ds(target * cap, cap)], arr.at[pl.ds(me * cap, cap)],
            rand_send.at[k], rand_recv.at[k], target,
        )

    def each(body, first=1, last=n):
        def step(k, c):
            body(k)
            return c
        lax.fori_loop(first, last, step, 0)

    each(lambda k: code(k).start())
    codes_in[pl.ds(me, 1)] = codes_ref[pl.ds(me, 1)]

    own_rows = pltpu.make_async_copy(w_ref, full_ref.at[me], local.at[0])
    own_rows.start()
    advance(0)

    tail = (blocks - 1) * block_len
    up, down = lax.rem(me + 1, n), lax.rem(me + n - 1, n)
    edges = []
    for i, ref in enumerate((k_hbm, v_hbm)):
        edges.append(remote(
            ref.at[tail : tail + block_len], low.at[i], edge_send.at[0, i], edge_recv.at[0, i], up
        ))
        edges.append(remote(
            ref.at[0:block_len], high.at[i], edge_send.at[1, i], edge_recv.at[1, i], down
        ))
    for copy in edges:
        copy.start()

    for copy in loads:
        copy.wait()
    for b in range(blocks):
        rows = slice(b * block_len, (b + 1) * block_len)
        for h in range(heads):
            cols = slice(h * head_dim, (h + 1) * head_dim)
            pairs[b * heads + h, :, 0:head_dim] = k_ref[rows, cols]
            pairs[b * heads + h, :, head_dim:wide] = v_ref[rows, cols]

    plane = 2 * y + x
    mates = ((0, 1), (1, 0), (1, 1))

    def mate(dy, dx):
        return lax.rem(y + dy, 2), lax.rem(x + dx, 2)

    def plane_cut(i):
        ty, tx = mate(*mates[i])
        return remote(
            cand.at[tx, pl.ds(ty * part, part)], got_p.at[plane], cut_send.at[i], cut_recv.at[i],
            z * 4 + ty * 2 + tx,
        )

    def line_give(dz):
        to = lax.rem(z + dz, lines)
        return remote(got_z.at[z], got_z.at[z], line_out.at[dz], line_in.at[dz], to * 4 + plane)

    def plane_give(i):
        ty, tx = mate(*mates[i])
        piece = shared.at[x, pl.ds(y * part, part)]
        return remote(piece, piece, give_send.at[i], give_recv.at[i], z * 4 + ty * 2 + tx)

    for g in range(2):
        base = glob_ref[g] % blocks * heads
        for h in range(heads):
            cand[g, h] = pairs[base + h]
    for i in range(3):
        plane_cut(i).start()
    got_p[plane] = cand[x, pl.ds(y * part, part)]
    holder = glob_ref[x] // blocks

    def globals_line():
        for i in range(3):
            plane_cut(i).wait_recv()
        got_z[z] = got_p[holder % 4]
        for dz in range(1, lines):
            line_give(dz).start()

    def globals_plane():
        for dz in range(1, lines):
            line_give(dz).wait_recv()
        shared[x, pl.ds(y * part, part)] = got_z[holder // 4]
        for i in range(3):
            plane_give(i).start()

    def globals_done():
        for i in range(3):
            plane_give(i).wait_recv()
        for copy in edges:
            copy.wait_recv()

    each(lambda k: code(k).wait_recv())
    to_smem = pltpu.make_async_copy(codes_in, codes, local.at[1])
    to_smem.start()
    to_smem.wait()

    def pack(target, out, place):
        for s in range(cap):
            out[place * cap + s] = pairs[codes[target, 0, s]]

    def ship(k):
        target = stride(k)
        pack(target, stage, target)
        rand(k).start()

    def begin(h, c):
        cols = pl.ds(pl.multiple_of(h * head_dim, head_dim), head_dim)
        kk = jnp.concatenate([low[0, :, cols], k_ref[:, cols], high[0, :, cols]], axis=0)
        vv = jnp.concatenate([low[1, :, cols], v_ref[:, cols], high[1, :, cols]], axis=0)
        kg = [shared[i, h, :, 0:head_dim] for i in range(2)]
        vg = [shared[i, h, :, head_dim:wide] for i in range(2)]
        for b in range(blocks):
            lo, hi = b * block_len, (b + 3) * block_len
            ks = jnp.concatenate([kk[lo:hi], *kg], axis=0)
            vs = jnp.concatenate([vv[lo:hi], *vg], axis=0)
            s = lax.dot_general(
                q_ref[lo : lo + block_len, cols], ks, (((1,), (1,)), ((), ())),
                preferred_element_type=jnp.float32,
            ) * scale
            top = jnp.max(s, axis=-1, keepdims=True)
            expo = jnp.exp(s - top)
            total = jnp.sum(expo, axis=-1, keepdims=True)
            rows = pl.ds(lo, block_len)
            acc[rows, cols] = jnp.dot(
                expo.astype(jnp.bfloat16), vs, preferred_element_type=jnp.float32
            )
            top_s[h, rows] = jnp.broadcast_to(top, (block_len, LANES))
            sum_s[h, rows] = jnp.broadcast_to(total, (block_len, LANES))
        return c

    def finish(h, c):
        cols = pl.ds(pl.multiple_of(h * head_dim, head_dim), head_dim)
        for b in range(blocks):
            e = b * heads + h
            pair = arr[slot_ref[e]]
            kr, vr = pair[:, 0:head_dim], pair[:, head_dim:wide]
            rows = pl.ds(b * block_len, block_len)
            s = lax.dot_general(
                q_ref[rows, cols], kr, (((1,), (1,)), ((), ())),
                preferred_element_type=jnp.float32,
            ) * scale
            before = top_s[h, rows, 0:1]
            top = jnp.maximum(before, jnp.max(s, axis=-1, keepdims=True))
            fade = jnp.exp(before - top)
            expo = jnp.exp(s - top)
            total = sum_s[h, rows, 0:1] * fade + jnp.sum(expo, axis=-1, keepdims=True)
            o = acc[rows, cols] * fade + jnp.dot(
                expo.astype(jnp.bfloat16), vr, preferred_element_type=jnp.float32
            )
            att[rows, cols] = (o * (1.0 / total)).astype(att.dtype)
        return c

    def attend(h0, h1):
        lax.fori_loop(h0, h1, begin, 0)

    third = n // 3
    each(ship, 1, 4)
    globals_line()
    advance(1)
    globals_plane()
    each(ship, 4, 8)
    forward(0)
    if lines > 2:
        advance(2)
    each(ship, 8, n)
    pack(me, arr, me)
    forward(1)
    globals_done()
    attend(0, 2)
    for t in range(3, lines):
        advance(t)
        if t == 3:
            attend(2, 4)
        forward(t - 1)
    attend(4, 6)
    forward(lines - 1)
    attend(6, heads)

    each(lambda k: rand(k).wait_recv())
    lax.fori_loop(0, heads, finish, 0)

    for t in range(lines):
        for side in sides(t):
            @pl.when(exists(side, t))
            def _():
                for way in (0, 1):
                    far(side, t, way).wait_recv()
    own_rows.wait()

    kept = out_ref.shape[0]
    depth = full_ref.shape[0] * full_ref.shape[1]
    step = give.shape[2]
    chunks = give.shape[0]

    def product(row, c):
        cols = pl.ds(pl.multiple_of(c * step, step), step)
        return jnp.dot(
            att[pl.ds(pl.multiple_of(row, kept), kept)],
            full_ref[:, :, cols].reshape(depth, step),
            preferred_element_type=jnp.float32,
        )

    def hand(c):
        return pltpu.make_async_remote_copy(
            src_ref=give.at[c], dst_ref=take.at[c], send_sem=core_send.at[c],
            recv_sem=core_recv.at[c], device_id={"head": 1 - hd}, device_id_type=MESH,
        )

    def theirs(c):
        give[c] = product((1 - hd) * kept, c).astype(give.dtype)
        hand(c).start()

    def ours(c):
        mine = product(hd * kept, c).astype(give.dtype).astype(jnp.float32)
        hand(c).wait_recv()
        cols = pl.ds(pl.multiple_of(c * step, step), step)
        out_ref[:, cols] = (mine + take[c].astype(jnp.float32)).astype(out_ref.dtype)

    each(theirs, 0, chunks)
    each(ours, 0, chunks)
    each(lambda c: hand(c).wait_send(), 0, chunks)

    for t in range(lines):
        for side in (0, 1):
            if t < lines - 1:
                @pl.when(passes(side, t))
                def _():
                    along(side, t).wait_send()
        for side in sides(t):
            @pl.when(exists(side, t))
            def _():
                for way in (0, 1):
                    near(side, t, way).wait_send()
                    far(side, t, way).wait_send()
    each(lambda k: code(k).wait_send())
    each(lambda k: rand(k).wait_send())
    for i in range(3):
        plane_cut(i).wait_send()
        plane_give(i).wait_send()
    for dz in range(1, lines):
        line_give(dz).wait_send()
    for copy in edges:
        copy.wait_send()


def layer(glob, places, codes, q, k, v, weight, n, cap, blocks, block_len, head_dim, heads):
    lines = n // 4
    rows, columns = weight.shape
    tokens, width = q.shape
    dma = pltpu.SemaphoreType.DMA
    vmem = pl.BlockSpec(memory_space=pltpu.VMEM)
    smem = pl.BlockSpec(memory_space=pltpu.SMEM)
    hbm = pl.BlockSpec(memory_space=pl.ANY)
    kind = q.dtype
    f32 = jnp.float32
    slots = (n * cap, block_len, 2 * head_dim)
    pair = (block_len, 2 * head_dim)
    chunks = 8
    return pl.pallas_call(
        functools.partial(
            layer_kernel, n, cap, blocks, block_len, head_dim, heads, head_dim ** (-0.5)
        ),
        out_shape=jax.ShapeDtypeStruct((tokens // 2, columns), kind),
        in_specs=[smem, smem, vmem, hbm, hbm, hbm, hbm],
        out_specs=vmem,
        scratch_shapes=[
            pltpu.VMEM(q.shape, kind),
            pltpu.VMEM(q.shape, kind),
            pltpu.VMEM(q.shape, kind),
            pltpu.VMEM((n, rows, columns), kind),
            pltpu.VMEM(q.shape, kind),
            pltpu.VMEM((chunks, tokens // 2, columns // chunks), kind),
            pltpu.VMEM((chunks, tokens // 2, columns // chunks), kind),
            pltpu.VMEM((blocks * heads, block_len, 2 * head_dim), kind),
            pltpu.VMEM(slots, kind),
            pltpu.VMEM(slots, kind),
            pltpu.VMEM(codes.shape, jnp.int32),
            pltpu.SMEM(codes.shape, jnp.int32),
            pltpu.VMEM((2, block_len, width), kind),
            pltpu.VMEM((2, block_len, width), kind),
            pltpu.VMEM((2, heads, *pair), kind),
            pltpu.VMEM((4, heads // 2, *pair), kind),
            pltpu.VMEM((lines, heads // 2, *pair), kind),
            pltpu.VMEM((2, heads, *pair), kind),
            pltpu.VMEM((tokens, width), f32),
            pltpu.VMEM((heads, tokens, LANES), f32),
            pltpu.VMEM((heads, tokens, LANES), f32),
            dma((2, lines)), dma((2, lines)),
            dma((2, lines, 2)), dma((2, lines, 2)),
            dma((2, lines, 2)), dma((2, lines, 2)),
            dma((n,)), dma((n,)), dma((n,)), dma((n,)),
            dma((2, 2)), dma((2, 2)),
            dma((3,)), dma((3,)), dma((lines,)), dma((lines,)), dma((3,)), dma((3,)),
            dma((chunks,)), dma((chunks,)), dma((5,)),
        ],
        compiler_params=pltpu.CompilerParams(
            collective_id=0, has_side_effects=True, vmem_limit_bytes=60 << 20
        ),
        cost_estimate=pl.CostEstimate(
            flops=4 * tokens * 6 * block_len * width,
            transcendentals=tokens * 6 * block_len * heads,
            bytes_accessed=40 * n * rows * columns,
        ),
        name="layer",
    )(glob, places, codes, q, k, v, weight)


def body(queries, keys, values, rand_blocks, global_blocks, out_weight):
    n = lax.axis_size("seq")
    block_count, head_count = rand_blocks.shape
    tokens, width = queries.shape
    block_len = tokens // block_count
    head_dim = width // head_count
    entries = block_count * head_count
    cap = max(2, (2 * entries + n - 1) // n)

    flat_blocks = rand_blocks.reshape(entries)
    owners = flat_blocks // block_count
    head_iota = jnp.arange(entries, dtype=jnp.int32) % head_count
    codes = flat_blocks % block_count * head_count + head_iota
    ranks = ranked(owners)
    target = jnp.arange(n, dtype=jnp.int32)[:, None, None]
    slot = jnp.arange(LANES, dtype=jnp.int32)[None, :, None]
    hits = (owners[None, None, :] == target) & (ranks[None, None, :] == slot)
    outgoing = jnp.sum(jnp.where(hits, codes[None, None, :], 0), axis=2)

    return layer(
        global_blocks, owners * cap + ranks, outgoing.reshape(n, 1, LANES), queries, keys, values,
        out_weight, n, cap, block_count, block_len, head_dim, head_count,
    )


def solution(mesh):
    placed = (
        P("seq", "head"),
        P("seq", "head"),
        P("seq", "head"),
        P("seq", "head"),
        P(),
        P(("head", "seq"), None),
    )
    return jax.shard_map(
        body, mesh=mesh, in_specs=placed, out_specs=P(("seq", "head"), None), check_vma=False
    )
```

```python
import functools

import jax
import jax.numpy as jnp
from jax import lax
from jax.experimental import pallas as pl
from jax.experimental.pallas import tpu as pltpu
from jax.sharding import PartitionSpec as P

MESH = pl.DeviceIdType.MESH
LANES = 128


def ranked(owners):
    count = owners.shape[0]
    order = jnp.arange(count, dtype=jnp.int32)
    earlier = (owners[:, None] == owners[None, :]) & (order[None, :] < order[:, None])
    return jnp.sum(earlier.astype(jnp.int32), axis=1)


def layer_kernel(
    n, cap, blocks, block_len, head_dim, heads, scale,
    glob_ref, slot_ref, codes_ref, q_hbm, k_hbm, v_hbm, w_ref,
    out_ref,
    q_ref, k_ref, v_ref, full_ref, att, give, take,
    pairs, stage, arr, codes_in, codes, low, high, cand, got_p, got_z, shared,
    acc, top_s, sum_s,
    line_send, line_recv, near_send, near_recv, far_send, far_recv,
    code_send, code_recv, rand_send, rand_recv, edge_send, edge_recv,
    cut_send, cut_recv, line_out, line_in, give_send, give_recv, core_send, core_recv, local,
):
    lines = n // 4
    me = lax.axis_index("seq")
    z, y, x = me // 4, me // 2 % 2, me % 2
    other_y = z * 4 + (1 - y) * 2 + x
    other_x = z * 4 + y * 2 + 1 - x
    half = w_ref.shape[1] // 2
    part = heads // 2
    wide = 2 * head_dim

    hd = lax.axis_index("head")
    loads = [
        pltpu.make_async_copy(src, dst, local.at[2 + i])
        for i, (src, dst) in enumerate(((k_hbm, k_ref), (v_hbm, v_ref), (q_hbm, q_ref)))
    ]
    for copy in loads:
        copy.start()

    barrier = pltpu.get_barrier_semaphore()

    def greet(k, c):
        pl.semaphore_signal(
            barrier, inc=1, device_id={"seq": lax.rem(me + k, n)}, device_id_type=MESH
        )
        return c

    lax.fori_loop(1, n, greet, 0)
    pl.semaphore_signal(barrier, inc=1, device_id={"head": 1 - hd}, device_id_type=MESH)
    pl.semaphore_wait(barrier, n)

    def remote(src, dst, send, recv, target):
        return pltpu.make_async_remote_copy(
            src_ref=src, dst_ref=dst, send_sem=send, recv_sem=recv,
            device_id={"seq": target}, device_id_type=MESH,
        )

    def origin(side, t):
        return (z - t if side == 0 else z + t) * 4

    def exists(side, t):
        return z - t >= 0 if side == 0 else z + t < lines

    def held(side, t):
        return w_ref if t == 0 else full_ref.at[origin(side, t) + y * 2 + x]

    def along(side, t):
        target = me + 4 if side == 0 else me - 4
        index = origin(side, t) + y * 2 + x
        return remote(
            held(side, t), full_ref.at[index], line_send.at[side, t], line_recv.at[side, t], target
        )

    def passes(side, t):
        ahead = z + 1 < lines if side == 0 else z >= 1
        return jnp.logical_and(exists(side, t), ahead)

    def near(side, t, way):
        index = origin(side, t) + y * 2 + x
        return remote(
            held(side, t), full_ref.at[index], near_send.at[side, t, way],
            near_recv.at[side, t, way], other_y if way == 0 else other_x,
        )

    def far(side, t, way):
        index = origin(side, t) + (
            (1 - y) * 2 + x if way == 0 else y * 2 + 1 - x
        )
        cols = pl.ds(way * half, half)
        return remote(
            full_ref.at[index, :, cols], full_ref.at[index, :, cols], far_send.at[side, t, way],
            far_recv.at[side, t, way], other_x if way == 0 else other_y,
        )

    def sides(t):
        return (0,) if t == 0 else (0, 1)

    def advance(t):
        for side in (0, 1):
            if t > 0:
                @pl.when(exists(side, t))
                def _():
                    along(side, t - 1).wait_recv()
            if t < lines - 1:
                @pl.when(passes(side, t))
                def _():
                    along(side, t).start()
        for side in sides(t):
            @pl.when(exists(side, t))
            def _():
                near(side, t, 0).start()
                near(side, t, 1).start()

    def forward(t):
        for side in sides(t):
            @pl.when(exists(side, t))
            def _():
                for way in (0, 1):
                    near(side, t, way).wait_recv()
                    far(side, t, way).start()

    def code(k):
        target = lax.rem(me + k, n)
        return remote(
            codes_ref.at[target], codes_in.at[me], code_send.at[k], code_recv.at[k], target
        )

    def stride(k):
        return lax.rem(me + lax.rem(k * (n // 2 - 1), n), n)

    def rand(k):
        target = stride(k)
        return remote(
            stage.at[pl.ds(target * cap, cap)], arr.at[pl.ds(me * cap, cap)],
            rand_send.at[k], rand_recv.at[k], target,
        )

    def each(body, first=1, last=n):
        def step(k, c):
            body(k)
            return c
        lax.fori_loop(first, last, step, 0)

    each(lambda k: code(k).start())
    codes_in[pl.ds(me, 1)] = codes_ref[pl.ds(me, 1)]

    own_rows = pltpu.make_async_copy(w_ref, full_ref.at[me], local.at[0])
    own_rows.start()
    advance(0)

    tail = (blocks - 1) * block_len
    up, down = lax.rem(me + 1, n), lax.rem(me + n - 1, n)
    edges = []
    for i, ref in enumerate((k_hbm, v_hbm)):
        edges.append(remote(
            ref.at[tail : tail + block_len], low.at[i], edge_send.at[0, i], edge_recv.at[0, i], up
        ))
        edges.append(remote(
            ref.at[0:block_len], high.at[i], edge_send.at[1, i], edge_recv.at[1, i], down
        ))
    for copy in edges:
        copy.start()

    for copy in loads:
        copy.wait()
    for b in range(blocks):
        rows = slice(b * block_len, (b + 1) * block_len)
        for h in range(heads):
            cols = slice(h * head_dim, (h + 1) * head_dim)
            pairs[b * heads + h, :, 0:head_dim] = k_ref[rows, cols]
            pairs[b * heads + h, :, head_dim:wide] = v_ref[rows, cols]

    plane = 2 * y + x
    mates = ((0, 1), (1, 0), (1, 1))

    def mate(dy, dx):
        return lax.rem(y + dy, 2), lax.rem(x + dx, 2)

    def plane_cut(i):
        ty, tx = mate(*mates[i])
        return remote(
            cand.at[tx, pl.ds(ty * part, part)], got_p.at[plane], cut_send.at[i], cut_recv.at[i],
            z * 4 + ty * 2 + tx,
        )

    def line_give(dz):
        to = lax.rem(z + dz, lines)
        return remote(got_z.at[z], got_z.at[z], line_out.at[dz], line_in.at[dz], to * 4 + plane)

    def plane_give(i):
        ty, tx = mate(*mates[i])
        piece = shared.at[x, pl.ds(y * part, part)]
        return remote(piece, piece, give_send.at[i], give_recv.at[i], z * 4 + ty * 2 + tx)

    for g in range(2):
        base = glob_ref[g] % blocks * heads
        for h in range(heads):
            cand[g, h] = pairs[base + h]
    for i in range(3):
        plane_cut(i).start()
    got_p[plane] = cand[x, pl.ds(y * part, part)]
    holder = glob_ref[x] // blocks

    def globals_line():
        for i in range(3):
            plane_cut(i).wait_recv()
        got_z[z] = got_p[holder % 4]
        for dz in range(1, lines):
            line_give(dz).start()

    def globals_plane():
        for dz in range(1, lines):
            line_give(dz).wait_recv()
        shared[x, pl.ds(y * part, part)] = got_z[holder // 4]
        for i in range(3):
            plane_give(i).start()

    def globals_done():
        for i in range(3):
            plane_give(i).wait_recv()
        for copy in edges:
            copy.wait_recv()

    each(lambda k: code(k).wait_recv())
    to_smem = pltpu.make_async_copy(codes_in, codes, local.at[1])
    to_smem.start()
    to_smem.wait()

    def pack(target, out, place):
        for s in range(cap):
            out[place * cap + s] = pairs[codes[target, 0, s]]

    def ship(k):
        target = stride(k)
        pack(target, stage, target)
        rand(k).start()

    def begin(h, c):
        cols = pl.ds(pl.multiple_of(h * head_dim, head_dim), head_dim)
        kk = jnp.concatenate([low[0, :, cols], k_ref[:, cols], high[0, :, cols]], axis=0)
        vv = jnp.concatenate([low[1, :, cols], v_ref[:, cols], high[1, :, cols]], axis=0)
        kg = [shared[i, h, :, 0:head_dim] for i in range(2)]
        vg = [shared[i, h, :, head_dim:wide] for i in range(2)]
        kg, vg = jnp.concatenate(kg, axis=0), jnp.concatenate(vg, axis=0)
        q = q_ref[:, cols]

        def against(rows, table):
            return lax.dot_general(
                rows, table, (((1,), (1,)), ((), ())), preferred_element_type=jnp.float32
            )

        def rows_of(array, b, count=1):
            return array[b * block_len : (b + count) * block_len]

        near_s = jnp.concatenate(
            [against(rows_of(q, b), rows_of(kk, b, 3)) for b in range(blocks)], axis=0
        ) * scale
        glob_s = against(q, kg) * scale
        top = jnp.maximum(
            jnp.max(near_s, axis=-1, keepdims=True), jnp.max(glob_s, axis=-1, keepdims=True)
        )
        near_e, glob_e = jnp.exp(near_s - top), jnp.exp(glob_s - top)
        total = jnp.sum(near_e, axis=-1, keepdims=True) + jnp.sum(glob_e, axis=-1, keepdims=True)
        near_w = near_e.astype(jnp.bfloat16)
        o = jnp.concatenate([
            jnp.dot(rows_of(near_w, b), rows_of(vv, b, 3), preferred_element_type=jnp.float32)
            for b in range(blocks)
        ], axis=0)
        acc[:, cols] = o + jnp.dot(
            glob_e.astype(jnp.bfloat16), vg, preferred_element_type=jnp.float32
        )
        top_s[h] = jnp.broadcast_to(top, top_s.shape[1:])
        sum_s[h] = jnp.broadcast_to(total, sum_s.shape[1:])
        return c

    def finish(h, c):
        cols = pl.ds(pl.multiple_of(h * head_dim, head_dim), head_dim)
        picked = [arr[slot_ref[b * heads + h]] for b in range(blocks)]
        s = jnp.concatenate([
            lax.dot_general(
                q_ref[b * block_len : (b + 1) * block_len, cols], pair[:, 0:head_dim],
                (((1,), (1,)), ((), ())), preferred_element_type=jnp.float32,
            )
            for b, pair in enumerate(picked)
        ], axis=0) * scale
        before = top_s[h]
        top = jnp.maximum(before, jnp.max(s, axis=-1, keepdims=True))
        fade = jnp.exp(before - top)
        expo = jnp.exp(s - top[:, 0:block_len])
        total = sum_s[h] * fade + jnp.sum(expo, axis=-1, keepdims=True)
        weight = expo.astype(jnp.bfloat16)
        o = jnp.concatenate([
            jnp.dot(
                weight[b * block_len : (b + 1) * block_len], pair[:, head_dim:wide],
                preferred_element_type=jnp.float32,
            )
            for b, pair in enumerate(picked)
        ], axis=0)
        att[:, cols] = ((acc[:, cols] * fade + o) * (1.0 / total)).astype(att.dtype)
        return c

    def attend(h0, h1):
        lax.fori_loop(h0, h1, begin, 0)

    third = n // 3
    each(ship, 1, 4)
    globals_line()
    advance(1)
    globals_plane()
    each(ship, 4, 8)
    forward(0)
    if lines > 2:
        advance(2)
    each(ship, 8, n)
    pack(me, arr, me)
    forward(1)
    globals_done()
    attend(0, 2)
    for t in range(3, lines):
        advance(t)
        if t == 3:
            attend(2, 4)
        forward(t - 1)
    attend(4, 6)
    forward(lines - 1)
    attend(6, heads)

    each(lambda k: rand(k).wait_recv())
    lax.fori_loop(0, heads, finish, 0)

    for t in range(lines):
        for side in sides(t):
            @pl.when(exists(side, t))
            def _():
                for way in (0, 1):
                    far(side, t, way).wait_recv()
    own_rows.wait()

    kept = out_ref.shape[0]
    depth = full_ref.shape[0] * full_ref.shape[1]
    step = give.shape[2]
    chunks = give.shape[0]

    def product(row, c):
        cols = pl.ds(pl.multiple_of(c * step, step), step)
        return jnp.dot(
            att[pl.ds(pl.multiple_of(row, kept), kept)],
            full_ref[:, :, cols].reshape(depth, step),
            preferred_element_type=jnp.float32,
        )

    def hand(c):
        return pltpu.make_async_remote_copy(
            src_ref=give.at[c], dst_ref=take.at[c], send_sem=core_send.at[c],
            recv_sem=core_recv.at[c], device_id={"head": 1 - hd}, device_id_type=MESH,
        )

    def theirs(c):
        give[c] = product((1 - hd) * kept, c).astype(give.dtype)
        hand(c).start()

    def ours(c):
        mine = product(hd * kept, c).astype(give.dtype).astype(jnp.float32)
        hand(c).wait_recv()
        cols = pl.ds(pl.multiple_of(c * step, step), step)
        out_ref[:, cols] = (mine + take[c].astype(jnp.float32)).astype(out_ref.dtype)

    each(theirs, 0, chunks)
    each(ours, 0, chunks)
    each(lambda c: hand(c).wait_send(), 0, chunks)

    for t in range(lines):
        for side in (0, 1):
            if t < lines - 1:
                @pl.when(passes(side, t))
                def _():
                    along(side, t).wait_send()
        for side in sides(t):
            @pl.when(exists(side, t))
            def _():
                for way in (0, 1):
                    near(side, t, way).wait_send()
                    far(side, t, way).wait_send()
    each(lambda k: code(k).wait_send())
    each(lambda k: rand(k).wait_send())
    for i in range(3):
        plane_cut(i).wait_send()
        plane_give(i).wait_send()
    for dz in range(1, lines):
        line_give(dz).wait_send()
    for copy in edges:
        copy.wait_send()


def layer(glob, places, codes, q, k, v, weight, n, cap, blocks, block_len, head_dim, heads):
    lines = n // 4
    rows, columns = weight.shape
    tokens, width = q.shape
    dma = pltpu.SemaphoreType.DMA
    vmem = pl.BlockSpec(memory_space=pltpu.VMEM)
    smem = pl.BlockSpec(memory_space=pltpu.SMEM)
    hbm = pl.BlockSpec(memory_space=pl.ANY)
    kind = q.dtype
    f32 = jnp.float32
    slots = (n * cap, block_len, 2 * head_dim)
    pair = (block_len, 2 * head_dim)
    chunks = 8
    return pl.pallas_call(
        functools.partial(
            layer_kernel, n, cap, blocks, block_len, head_dim, heads, head_dim ** (-0.5)
        ),
        out_shape=jax.ShapeDtypeStruct((tokens // 2, columns), kind),
        in_specs=[smem, smem, vmem, hbm, hbm, hbm, hbm],
        out_specs=vmem,
        scratch_shapes=[
            pltpu.VMEM(q.shape, kind),
            pltpu.VMEM(q.shape, kind),
            pltpu.VMEM(q.shape, kind),
            pltpu.VMEM((n, rows, columns), kind),
            pltpu.VMEM(q.shape, kind),
            pltpu.VMEM((chunks, tokens // 2, columns // chunks), kind),
            pltpu.VMEM((chunks, tokens // 2, columns // chunks), kind),
            pltpu.VMEM((blocks * heads, block_len, 2 * head_dim), kind),
            pltpu.VMEM(slots, kind),
            pltpu.VMEM(slots, kind),
            pltpu.VMEM(codes.shape, jnp.int32),
            pltpu.SMEM(codes.shape, jnp.int32),
            pltpu.VMEM((2, block_len, width), kind),
            pltpu.VMEM((2, block_len, width), kind),
            pltpu.VMEM((2, heads, *pair), kind),
            pltpu.VMEM((4, heads // 2, *pair), kind),
            pltpu.VMEM((lines, heads // 2, *pair), kind),
            pltpu.VMEM((2, heads, *pair), kind),
            pltpu.VMEM((tokens, width), f32),
            pltpu.VMEM((heads, tokens, LANES), f32),
            pltpu.VMEM((heads, tokens, LANES), f32),
            dma((2, lines)), dma((2, lines)),
            dma((2, lines, 2)), dma((2, lines, 2)),
            dma((2, lines, 2)), dma((2, lines, 2)),
            dma((n,)), dma((n,)), dma((n,)), dma((n,)),
            dma((2, 2)), dma((2, 2)),
            dma((3,)), dma((3,)), dma((lines,)), dma((lines,)), dma((3,)), dma((3,)),
            dma((chunks,)), dma((chunks,)), dma((5,)),
        ],
        compiler_params=pltpu.CompilerParams(
            collective_id=0, has_side_effects=True, vmem_limit_bytes=60 << 20
        ),
        cost_estimate=pl.CostEstimate(
            flops=4 * tokens * 6 * block_len * width,
            transcendentals=tokens * 6 * block_len * heads,
            bytes_accessed=40 * n * rows * columns,
        ),
        name="layer",
    )(glob, places, codes, q, k, v, weight)


def body(queries, keys, values, rand_blocks, global_blocks, out_weight):
    n = lax.axis_size("seq")
    block_count, head_count = rand_blocks.shape
    tokens, width = queries.shape
    block_len = tokens // block_count
    head_dim = width // head_count
    entries = block_count * head_count
    cap = max(2, (2 * entries + n - 1) // n)

    flat_blocks = rand_blocks.reshape(entries)
    owners = flat_blocks // block_count
    head_iota = jnp.arange(entries, dtype=jnp.int32) % head_count
    codes = flat_blocks % block_count * head_count + head_iota
    ranks = ranked(owners)
    target = jnp.arange(n, dtype=jnp.int32)[:, None, None]
    slot = jnp.arange(LANES, dtype=jnp.int32)[None, :, None]
    hits = (owners[None, None, :] == target) & (ranks[None, None, :] == slot)
    outgoing = jnp.sum(jnp.where(hits, codes[None, None, :], 0), axis=2)

    return layer(
        global_blocks, owners * cap + ranks, outgoing.reshape(n, 1, LANES), queries, keys, values,
        out_weight, n, cap, block_count, block_len, head_dim, head_count,
    )


def solution(mesh):
    placed = (
        P("seq", "head"),
        P("seq", "head"),
        P("seq", "head"),
        P("seq", "head"),
        P(),
        P(("head", "seq"), None),
    )
    return jax.shard_map(
        body, mesh=mesh, in_specs=placed, out_specs=P(("seq", "head"), None), check_vma=False
    )
```

```python
import functools

import jax
import jax.numpy as jnp
from jax import lax
from jax.experimental import pallas as pl
from jax.experimental.pallas import tpu as pltpu
from jax.sharding import PartitionSpec as P

MESH = pl.DeviceIdType.MESH
LANES = 128


def ranked(owners):
    count = owners.shape[0]
    order = jnp.arange(count, dtype=jnp.int32)
    earlier = (owners[:, None] == owners[None, :]) & (order[None, :] < order[:, None])
    return jnp.sum(earlier.astype(jnp.int32), axis=1)


def layer_kernel(
    n, cap, blocks, block_len, head_dim, heads, scale,
    glob_ref, slot_ref, codes_ref, q_hbm, k_hbm, v_hbm, w_ref,
    out_ref,
    q_ref, k_ref, v_ref, full_ref, att, give, take,
    pairs, stage, arr, codes_in, codes, low, high, cand, got_p, got_z, shared,
    acc, top_s, sum_s,
    line_send, line_recv, near_send, near_recv, far_send, far_recv,
    code_send, code_recv, rand_send, rand_recv, edge_send, edge_recv,
    cut_send, cut_recv, line_out, line_in, give_send, give_recv, core_send, core_recv, local,
):
    lines = n // 4
    me = lax.axis_index("seq")
    z, y, x = me // 4, me // 2 % 2, me % 2
    other_y = z * 4 + (1 - y) * 2 + x
    other_x = z * 4 + y * 2 + 1 - x
    half = w_ref.shape[1] // 2
    part = heads // 2
    wide = 2 * head_dim

    hd = lax.axis_index("head")
    loads = [
        pltpu.make_async_copy(src, dst, local.at[2 + i])
        for i, (src, dst) in enumerate(((k_hbm, k_ref), (v_hbm, v_ref), (q_hbm, q_ref)))
    ]
    for copy in loads:
        copy.start()

    barrier = pltpu.get_barrier_semaphore()

    def greet(k, c):
        pl.semaphore_signal(
            barrier, inc=1, device_id={"seq": lax.rem(me + k, n)}, device_id_type=MESH
        )
        return c

    lax.fori_loop(1, n, greet, 0)
    pl.semaphore_signal(barrier, inc=1, device_id={"head": 1 - hd}, device_id_type=MESH)
    pl.semaphore_wait(barrier, n)

    def remote(src, dst, send, recv, target):
        return pltpu.make_async_remote_copy(
            src_ref=src, dst_ref=dst, send_sem=send, recv_sem=recv,
            device_id={"seq": target}, device_id_type=MESH,
        )

    def origin(side, t):
        return (z - t if side == 0 else z + t) * 4

    def exists(side, t):
        return z - t >= 0 if side == 0 else z + t < lines

    def held(side, t):
        return w_ref if t == 0 else full_ref.at[origin(side, t) + y * 2 + x]

    def along(side, t):
        target = me + 4 if side == 0 else me - 4
        index = origin(side, t) + y * 2 + x
        return remote(
            held(side, t), full_ref.at[index], line_send.at[side, t], line_recv.at[side, t], target
        )

    def passes(side, t):
        ahead = z + 1 < lines if side == 0 else z >= 1
        return jnp.logical_and(exists(side, t), ahead)

    def near(side, t, way):
        index = origin(side, t) + y * 2 + x
        return remote(
            held(side, t), full_ref.at[index], near_send.at[side, t, way],
            near_recv.at[side, t, way], other_y if way == 0 else other_x,
        )

    def far(side, t, way):
        index = origin(side, t) + (
            (1 - y) * 2 + x if way == 0 else y * 2 + 1 - x
        )
        cols = pl.ds(way * half, half)
        return remote(
            full_ref.at[index, :, cols], full_ref.at[index, :, cols], far_send.at[side, t, way],
            far_recv.at[side, t, way], other_x if way == 0 else other_y,
        )

    def sides(t):
        return (0,) if t == 0 else (0, 1)

    def advance(t):
        for side in (0, 1):
            if t > 0:
                @pl.when(exists(side, t))
                def _():
                    along(side, t - 1).wait_recv()
            if t < lines - 1:
                @pl.when(passes(side, t))
                def _():
                    along(side, t).start()
        for side in sides(t):
            @pl.when(exists(side, t))
            def _():
                near(side, t, 0).start()
                near(side, t, 1).start()

    def forward(t):
        for side in sides(t):
            @pl.when(exists(side, t))
            def _():
                for way in (0, 1):
                    near(side, t, way).wait_recv()
                    far(side, t, way).start()

    def code(k):
        target = lax.rem(me + k, n)
        return remote(
            codes_ref.at[target], codes_in.at[me], code_send.at[k], code_recv.at[k], target
        )

    def stride(k):
        return lax.rem(me + lax.rem(k * (n // 2 - 1), n), n)

    def rand(k):
        target = stride(k)
        return remote(
            stage.at[pl.ds(target * cap, cap)], arr.at[pl.ds(me * cap, cap)],
            rand_send.at[k], rand_recv.at[k], target,
        )

    def each(body, first=1, last=n):
        def step(k, c):
            body(k)
            return c
        lax.fori_loop(first, last, step, 0)

    each(lambda k: code(k).start())
    codes_in[pl.ds(me, 1)] = codes_ref[pl.ds(me, 1)]

    own_rows = pltpu.make_async_copy(w_ref, full_ref.at[me], local.at[0])
    own_rows.start()
    advance(0)

    tail = (blocks - 1) * block_len
    up, down = lax.rem(me + 1, n), lax.rem(me + n - 1, n)
    edges = []
    for i, ref in enumerate((k_hbm, v_hbm)):
        edges.append(remote(
            ref.at[tail : tail + block_len], low.at[i], edge_send.at[0, i], edge_recv.at[0, i], up
        ))
        edges.append(remote(
            ref.at[0:block_len], high.at[i], edge_send.at[1, i], edge_recv.at[1, i], down
        ))
    for copy in edges:
        copy.start()

    for copy in loads:
        copy.wait()
    for b in range(blocks):
        rows = slice(b * block_len, (b + 1) * block_len)
        for h in range(heads):
            cols = slice(h * head_dim, (h + 1) * head_dim)
            pairs[b * heads + h, :, 0:head_dim] = k_ref[rows, cols]
            pairs[b * heads + h, :, head_dim:wide] = v_ref[rows, cols]

    plane = 2 * y + x
    mates = ((0, 1), (1, 0), (1, 1))

    def mate(dy, dx):
        return lax.rem(y + dy, 2), lax.rem(x + dx, 2)

    def plane_cut(i):
        ty, tx = mate(*mates[i])
        return remote(
            cand.at[tx, pl.ds(ty * part, part)], got_p.at[plane], cut_send.at[i], cut_recv.at[i],
            z * 4 + ty * 2 + tx,
        )

    def line_give(dz):
        to = lax.rem(z + dz, lines)
        return remote(got_z.at[z], got_z.at[z], line_out.at[dz], line_in.at[dz], to * 4 + plane)

    def plane_give(i):
        ty, tx = mate(*mates[i])
        piece = shared.at[x, pl.ds(y * part, part)]
        return remote(piece, piece, give_send.at[i], give_recv.at[i], z * 4 + ty * 2 + tx)

    for g in range(2):
        base = glob_ref[g] % blocks * heads
        for h in range(heads):
            cand[g, h] = pairs[base + h]
    for i in range(3):
        plane_cut(i).start()
    got_p[plane] = cand[x, pl.ds(y * part, part)]
    holder = glob_ref[x] // blocks

    def globals_line():
        for i in range(3):
            plane_cut(i).wait_recv()
        got_z[z] = got_p[holder % 4]
        for dz in range(1, lines):
            line_give(dz).start()

    def globals_plane():
        for dz in range(1, lines):
            line_give(dz).wait_recv()
        shared[x, pl.ds(y * part, part)] = got_z[holder // 4]
        for i in range(3):
            plane_give(i).start()

    def globals_done():
        for i in range(3):
            plane_give(i).wait_recv()
        for copy in edges:
            copy.wait_recv()

    each(lambda k: code(k).wait_recv())
    to_smem = pltpu.make_async_copy(codes_in, codes, local.at[1])
    to_smem.start()
    to_smem.wait()

    def pack(target, out, place):
        for s in range(cap):
            out[place * cap + s] = pairs[codes[target, 0, s]]

    def ship(k):
        target = stride(k)
        pack(target, stage, target)
        rand(k).start()

    def begin(h, c):
        cols = pl.ds(pl.multiple_of(h * head_dim, head_dim), head_dim)
        kk = jnp.concatenate([low[0, :, cols], k_ref[:, cols], high[0, :, cols]], axis=0)
        vv = jnp.concatenate([low[1, :, cols], v_ref[:, cols], high[1, :, cols]], axis=0)
        kg = [shared[i, h, :, 0:head_dim] for i in range(2)]
        vg = [shared[i, h, :, head_dim:wide] for i in range(2)]
        kg, vg = jnp.concatenate(kg, axis=0), jnp.concatenate(vg, axis=0)
        q = q_ref[:, cols]

        def against(rows, table):
            return lax.dot_general(
                rows, table, (((1,), (1,)), ((), ())), preferred_element_type=jnp.float32
            )

        def rows_of(array, b, count=1):
            return array[b * block_len : (b + count) * block_len]

        near_s = jnp.concatenate(
            [against(rows_of(q, b), rows_of(kk, b, 3)) for b in range(blocks)], axis=0
        ) * scale
        glob_s = against(q, kg) * scale
        top = jnp.maximum(
            jnp.max(near_s, axis=-1, keepdims=True), jnp.max(glob_s, axis=-1, keepdims=True)
        )
        near_e, glob_e = jnp.exp(near_s - top), jnp.exp(glob_s - top)
        total = jnp.sum(near_e, axis=-1, keepdims=True) + jnp.sum(glob_e, axis=-1, keepdims=True)
        near_w = near_e.astype(jnp.bfloat16)
        o = jnp.concatenate([
            jnp.dot(rows_of(near_w, b), rows_of(vv, b, 3), preferred_element_type=jnp.float32)
            for b in range(blocks)
        ], axis=0)
        acc[:, cols] = o + jnp.dot(
            glob_e.astype(jnp.bfloat16), vg, preferred_element_type=jnp.float32
        )
        top_s[h] = jnp.broadcast_to(top, top_s.shape[1:])
        sum_s[h] = jnp.broadcast_to(total, sum_s.shape[1:])
        return c

    def finish(h, c):
        cols = pl.ds(pl.multiple_of(h * head_dim, head_dim), head_dim)
        picked = [arr[slot_ref[b * heads + h]] for b in range(blocks)]
        s = jnp.concatenate([
            lax.dot_general(
                q_ref[b * block_len : (b + 1) * block_len, cols], pair[:, 0:head_dim],
                (((1,), (1,)), ((), ())), preferred_element_type=jnp.float32,
            )
            for b, pair in enumerate(picked)
        ], axis=0) * scale
        before = top_s[h]
        top = jnp.maximum(before, jnp.max(s, axis=-1, keepdims=True))
        fade = jnp.exp(before - top)
        expo = jnp.exp(s - top[:, 0:block_len])
        total = sum_s[h] * fade + jnp.sum(expo, axis=-1, keepdims=True)
        weight = expo.astype(jnp.bfloat16)
        o = jnp.concatenate([
            jnp.dot(
                weight[b * block_len : (b + 1) * block_len], pair[:, head_dim:wide],
                preferred_element_type=jnp.float32,
            )
            for b, pair in enumerate(picked)
        ], axis=0)
        att[:, cols] = ((acc[:, cols] * fade + o) * (1.0 / total)).astype(att.dtype)
        return c

    def attend(h0, h1):
        lax.fori_loop(h0, h1, begin, 0)

    each(ship, 1, n // 4)
    advance(1)
    globals_line()
    each(ship, n // 4, n // 2)
    forward(0)
    if lines > 2:
        advance(2)
    globals_plane()
    each(ship, n // 2, n)
    pack(me, arr, me)
    forward(1)
    for t in range(3, lines):
        advance(t)
        if t == 3:
            globals_done()
        forward(t - 1)
    attend(0, heads // 2)
    forward(lines - 1)
    attend(heads // 2, heads)

    each(lambda k: rand(k).wait_recv())
    lax.fori_loop(0, heads, finish, 0)

    for t in range(lines):
        for side in sides(t):
            @pl.when(exists(side, t))
            def _():
                for way in (0, 1):
                    far(side, t, way).wait_recv()
    own_rows.wait()

    kept = out_ref.shape[0]
    depth = full_ref.shape[0] * full_ref.shape[1]
    step = give.shape[2]
    chunks = give.shape[0]

    def product(row, c):
        cols = pl.ds(pl.multiple_of(c * step, step), step)
        return jnp.dot(
            att[pl.ds(pl.multiple_of(row, kept), kept)],
            full_ref[:, :, cols].reshape(depth, step),
            preferred_element_type=jnp.float32,
        )

    def hand(c):
        return pltpu.make_async_remote_copy(
            src_ref=give.at[c], dst_ref=take.at[c], send_sem=core_send.at[c],
            recv_sem=core_recv.at[c], device_id={"head": 1 - hd}, device_id_type=MESH,
        )

    def theirs(c):
        give[c] = product((1 - hd) * kept, c).astype(give.dtype)
        hand(c).start()

    def ours(c):
        mine = product(hd * kept, c).astype(give.dtype).astype(jnp.float32)
        hand(c).wait_recv()
        cols = pl.ds(pl.multiple_of(c * step, step), step)
        out_ref[:, cols] = (mine + take[c].astype(jnp.float32)).astype(out_ref.dtype)

    each(theirs, 0, chunks)
    each(ours, 0, chunks)
    each(lambda c: hand(c).wait_send(), 0, chunks)

    for t in range(lines):
        for side in (0, 1):
            if t < lines - 1:
                @pl.when(passes(side, t))
                def _():
                    along(side, t).wait_send()
        for side in sides(t):
            @pl.when(exists(side, t))
            def _():
                for way in (0, 1):
                    near(side, t, way).wait_send()
                    far(side, t, way).wait_send()
    each(lambda k: code(k).wait_send())
    each(lambda k: rand(k).wait_send())
    for i in range(3):
        plane_cut(i).wait_send()
        plane_give(i).wait_send()
    for dz in range(1, lines):
        line_give(dz).wait_send()
    for copy in edges:
        copy.wait_send()


def layer(glob, places, codes, q, k, v, weight, n, cap, blocks, block_len, head_dim, heads):
    lines = n // 4
    rows, columns = weight.shape
    tokens, width = q.shape
    dma = pltpu.SemaphoreType.DMA
    vmem = pl.BlockSpec(memory_space=pltpu.VMEM)
    smem = pl.BlockSpec(memory_space=pltpu.SMEM)
    hbm = pl.BlockSpec(memory_space=pl.ANY)
    kind = q.dtype
    f32 = jnp.float32
    slots = (n * cap, block_len, 2 * head_dim)
    pair = (block_len, 2 * head_dim)
    chunks = 8
    return pl.pallas_call(
        functools.partial(
            layer_kernel, n, cap, blocks, block_len, head_dim, heads, head_dim ** (-0.5)
        ),
        out_shape=jax.ShapeDtypeStruct((tokens // 2, columns), kind),
        in_specs=[smem, smem, vmem, hbm, hbm, hbm, hbm],
        out_specs=vmem,
        scratch_shapes=[
            pltpu.VMEM(q.shape, kind),
            pltpu.VMEM(q.shape, kind),
            pltpu.VMEM(q.shape, kind),
            pltpu.VMEM((n, rows, columns), kind),
            pltpu.VMEM(q.shape, kind),
            pltpu.VMEM((chunks, tokens // 2, columns // chunks), kind),
            pltpu.VMEM((chunks, tokens // 2, columns // chunks), kind),
            pltpu.VMEM((blocks * heads, block_len, 2 * head_dim), kind),
            pltpu.VMEM(slots, kind),
            pltpu.VMEM(slots, kind),
            pltpu.VMEM(codes.shape, jnp.int32),
            pltpu.SMEM(codes.shape, jnp.int32),
            pltpu.VMEM((2, block_len, width), kind),
            pltpu.VMEM((2, block_len, width), kind),
            pltpu.VMEM((2, heads, *pair), kind),
            pltpu.VMEM((4, heads // 2, *pair), kind),
            pltpu.VMEM((lines, heads // 2, *pair), kind),
            pltpu.VMEM((2, heads, *pair), kind),
            pltpu.VMEM((tokens, width), f32),
            pltpu.VMEM((heads, tokens, LANES), f32),
            pltpu.VMEM((heads, tokens, LANES), f32),
            dma((2, lines)), dma((2, lines)),
            dma((2, lines, 2)), dma((2, lines, 2)),
            dma((2, lines, 2)), dma((2, lines, 2)),
            dma((n,)), dma((n,)), dma((n,)), dma((n,)),
            dma((2, 2)), dma((2, 2)),
            dma((3,)), dma((3,)), dma((lines,)), dma((lines,)), dma((3,)), dma((3,)),
            dma((chunks,)), dma((chunks,)), dma((5,)),
        ],
        compiler_params=pltpu.CompilerParams(
            collective_id=0, has_side_effects=True, vmem_limit_bytes=60 << 20
        ),
        cost_estimate=pl.CostEstimate(
            flops=4 * tokens * 6 * block_len * width,
            transcendentals=tokens * 6 * block_len * heads,
            bytes_accessed=40 * n * rows * columns,
        ),
        name="layer",
    )(glob, places, codes, q, k, v, weight)


def body(queries, keys, values, rand_blocks, global_blocks, out_weight):
    n = lax.axis_size("seq")
    block_count, head_count = rand_blocks.shape
    tokens, width = queries.shape
    block_len = tokens // block_count
    head_dim = width // head_count
    entries = block_count * head_count
    cap = max(2, (2 * entries + n - 1) // n)

    flat_blocks = rand_blocks.reshape(entries)
    owners = flat_blocks // block_count
    head_iota = jnp.arange(entries, dtype=jnp.int32) % head_count
    codes = flat_blocks % block_count * head_count + head_iota
    ranks = ranked(owners)
    target = jnp.arange(n, dtype=jnp.int32)[:, None, None]
    slot = jnp.arange(LANES, dtype=jnp.int32)[None, :, None]
    hits = (owners[None, None, :] == target) & (ranks[None, None, :] == slot)
    outgoing = jnp.sum(jnp.where(hits, codes[None, None, :], 0), axis=2)

    return layer(
        global_blocks, owners * cap + ranks, outgoing.reshape(n, 1, LANES), queries, keys, values,
        out_weight, n, cap, block_count, block_len, head_dim, head_count,
    )


def solution(mesh):
    placed = (
        P("seq", "head"),
        P("seq", "head"),
        P("seq", "head"),
        P("seq", "head"),
        P(),
        P(("head", "seq"), None),
    )
    return jax.shard_map(
        body, mesh=mesh, in_specs=placed, out_specs=P(("seq", "head"), None), check_vma=False
    )
```

```python
import functools

import jax
import jax.numpy as jnp
from jax import lax
from jax.experimental import pallas as pl
from jax.experimental.pallas import tpu as pltpu
from jax.sharding import PartitionSpec as P

MESH = pl.DeviceIdType.MESH
LANES = 128


def ranked(owners):
    count = owners.shape[0]
    order = jnp.arange(count, dtype=jnp.int32)
    earlier = (owners[:, None] == owners[None, :]) & (order[None, :] < order[:, None])
    return jnp.sum(earlier.astype(jnp.int32), axis=1)


def layer_kernel(
    n, cap, blocks, block_len, head_dim, heads, scale,
    glob_ref, slot_ref, codes_ref, q_hbm, k_hbm, v_hbm, w_ref,
    out_ref,
    q_ref, k_ref, v_ref, full_ref, att, give, take,
    pairs, stage, arr, codes_in, codes, low, high, cand, got_p, got_z, shared,
    acc, top_s, sum_s,
    line_send, line_recv, near_send, near_recv, far_send, far_recv,
    code_send, code_recv, rand_send, rand_recv, edge_send, edge_recv,
    cut_send, cut_recv, line_out, line_in, give_send, give_recv, core_send, core_recv, local,
):
    lines = n // 4
    me = lax.axis_index("seq")
    z, y, x = me // 4, me // 2 % 2, me % 2
    other_y = z * 4 + (1 - y) * 2 + x
    other_x = z * 4 + y * 2 + 1 - x
    half = w_ref.shape[1] // 2
    part = heads // 2
    wide = 2 * head_dim

    hd = lax.axis_index("head")
    loads = [
        pltpu.make_async_copy(src, dst, local.at[2 + i])
        for i, (src, dst) in enumerate(((k_hbm, k_ref), (v_hbm, v_ref), (q_hbm, q_ref)))
    ]
    for copy in loads:
        copy.start()

    barrier = pltpu.get_barrier_semaphore()

    def greet(k, c):
        pl.semaphore_signal(
            barrier, inc=1, device_id={"seq": lax.rem(me + k, n)}, device_id_type=MESH
        )
        return c

    lax.fori_loop(1, n, greet, 0)
    pl.semaphore_signal(barrier, inc=1, device_id={"head": 1 - hd}, device_id_type=MESH)
    pl.semaphore_wait(barrier, n)

    def remote(src, dst, send, recv, target):
        return pltpu.make_async_remote_copy(
            src_ref=src, dst_ref=dst, send_sem=send, recv_sem=recv,
            device_id={"seq": target}, device_id_type=MESH,
        )

    def origin(side, t):
        return (z - t if side == 0 else z + t) * 4

    def exists(side, t):
        return z - t >= 0 if side == 0 else z + t < lines

    def held(side, t):
        return w_ref if t == 0 else full_ref.at[origin(side, t) + y * 2 + x]

    def along(side, t):
        target = me + 4 if side == 0 else me - 4
        index = origin(side, t) + y * 2 + x
        return remote(
            held(side, t), full_ref.at[index], line_send.at[side, t], line_recv.at[side, t], target
        )

    def passes(side, t):
        ahead = z + 1 < lines if side == 0 else z >= 1
        return jnp.logical_and(exists(side, t), ahead)

    def near(side, t, way):
        index = origin(side, t) + y * 2 + x
        return remote(
            held(side, t), full_ref.at[index], near_send.at[side, t, way],
            near_recv.at[side, t, way], other_y if way == 0 else other_x,
        )

    def far(side, t, way):
        index = origin(side, t) + (
            (1 - y) * 2 + x if way == 0 else y * 2 + 1 - x
        )
        cols = pl.ds(way * half, half)
        return remote(
            full_ref.at[index, :, cols], full_ref.at[index, :, cols], far_send.at[side, t, way],
            far_recv.at[side, t, way], other_x if way == 0 else other_y,
        )

    def sides(t):
        return (0,) if t == 0 else (0, 1)

    def advance(t):
        for side in (0, 1):
            if t > 0:
                @pl.when(exists(side, t))
                def _():
                    along(side, t - 1).wait_recv()
            if t < lines - 1:
                @pl.when(passes(side, t))
                def _():
                    along(side, t).start()
        for side in sides(t):
            @pl.when(exists(side, t))
            def _():
                near(side, t, 0).start()
                near(side, t, 1).start()

    def forward(t):
        for side in sides(t):
            @pl.when(exists(side, t))
            def _():
                for way in (0, 1):
                    near(side, t, way).wait_recv()
                    far(side, t, way).start()

    def code(k):
        target = lax.rem(me + k, n)
        return remote(
            codes_ref.at[target], codes_in.at[me], code_send.at[k], code_recv.at[k], target
        )

    def stride(k):
        return lax.rem(me + lax.rem(k * (n // 2 - 1), n), n)

    def rand(k):
        target = stride(k)
        return remote(
            stage.at[pl.ds(target * cap, cap)], arr.at[pl.ds(me * cap, cap)],
            rand_send.at[k], rand_recv.at[k], target,
        )

    def each(body, first=1, last=n):
        def step(k, c):
            body(k)
            return c
        lax.fori_loop(first, last, step, 0)

    each(lambda k: code(k).start())
    codes_in[pl.ds(me, 1)] = codes_ref[pl.ds(me, 1)]

    own_rows = pltpu.make_async_copy(w_ref, full_ref.at[me], local.at[0])
    own_rows.start()
    advance(0)

    tail = (blocks - 1) * block_len
    up, down = lax.rem(me + 1, n), lax.rem(me + n - 1, n)
    edges = []
    for i, ref in enumerate((k_hbm, v_hbm)):
        edges.append(remote(
            ref.at[tail : tail + block_len], low.at[i], edge_send.at[0, i], edge_recv.at[0, i], up
        ))
        edges.append(remote(
            ref.at[0:block_len], high.at[i], edge_send.at[1, i], edge_recv.at[1, i], down
        ))
    for copy in edges:
        copy.start()

    for copy in loads:
        copy.wait()
    for b in range(blocks):
        rows = slice(b * block_len, (b + 1) * block_len)
        for h in range(heads):
            cols = slice(h * head_dim, (h + 1) * head_dim)
            pairs[b * heads + h, :, 0:head_dim] = k_ref[rows, cols]
            pairs[b * heads + h, :, head_dim:wide] = v_ref[rows, cols]

    plane = 2 * y + x
    mates = ((0, 1), (1, 0), (1, 1))

    def mate(dy, dx):
        return lax.rem(y + dy, 2), lax.rem(x + dx, 2)

    def plane_cut(i):
        ty, tx = mate(*mates[i])
        return remote(
            cand.at[tx, pl.ds(ty * part, part)], got_p.at[plane], cut_send.at[i], cut_recv.at[i],
            z * 4 + ty * 2 + tx,
        )

    def line_give(dz):
        to = lax.rem(z + dz, lines)
        return remote(got_z.at[z], got_z.at[z], line_out.at[dz], line_in.at[dz], to * 4 + plane)

    def plane_give(i):
        ty, tx = mate(*mates[i])
        piece = shared.at[x, pl.ds(y * part, part)]
        return remote(piece, piece, give_send.at[i], give_recv.at[i], z * 4 + ty * 2 + tx)

    for g in range(2):
        base = glob_ref[g] % blocks * heads
        for h in range(heads):
            cand[g, h] = pairs[base + h]
    for i in range(3):
        plane_cut(i).start()
    got_p[plane] = cand[x, pl.ds(y * part, part)]
    holder = glob_ref[x] // blocks

    def globals_line():
        for i in range(3):
            plane_cut(i).wait_recv()
        got_z[z] = got_p[holder % 4]
        for dz in range(1, lines):
            line_give(dz).start()

    def globals_plane():
        for dz in range(1, lines):
            line_give(dz).wait_recv()
        shared[x, pl.ds(y * part, part)] = got_z[holder // 4]
        for i in range(3):
            plane_give(i).start()

    def globals_done():
        for i in range(3):
            plane_give(i).wait_recv()
        for copy in edges:
            copy.wait_recv()

    each(lambda k: code(k).wait_recv())
    to_smem = pltpu.make_async_copy(codes_in, codes, local.at[1])
    to_smem.start()
    to_smem.wait()

    def pack(target, out, place):
        for s in range(cap):
            out[place * cap + s] = pairs[codes[target, 0, s]]

    def ship(k):
        target = stride(k)
        pack(target, stage, target)
        rand(k).start()

    def begin(h, c):
        cols = pl.ds(pl.multiple_of(h * head_dim, head_dim), head_dim)
        kk = jnp.concatenate([low[0, :, cols], k_ref[:, cols], high[0, :, cols]], axis=0)
        vv = jnp.concatenate([low[1, :, cols], v_ref[:, cols], high[1, :, cols]], axis=0)
        kg = [shared[i, h, :, 0:head_dim] for i in range(2)]
        vg = [shared[i, h, :, head_dim:wide] for i in range(2)]
        kg, vg = jnp.concatenate(kg, axis=0), jnp.concatenate(vg, axis=0)
        q = q_ref[:, cols]

        def against(rows, table):
            return lax.dot_general(
                rows, table, (((1,), (1,)), ((), ())), preferred_element_type=jnp.float32
            )

        def rows_of(array, b, count=1):
            return array[b * block_len : (b + count) * block_len]

        near_s = jnp.concatenate(
            [against(rows_of(q, b), rows_of(kk, b, 3)) for b in range(blocks)], axis=0
        ) * scale
        glob_s = against(q, kg) * scale
        top = jnp.maximum(
            jnp.max(near_s, axis=-1, keepdims=True), jnp.max(glob_s, axis=-1, keepdims=True)
        )
        near_e, glob_e = jnp.exp(near_s - top), jnp.exp(glob_s - top)
        total = jnp.sum(near_e, axis=-1, keepdims=True) + jnp.sum(glob_e, axis=-1, keepdims=True)
        near_w = near_e.astype(jnp.bfloat16)
        o = jnp.concatenate([
            jnp.dot(rows_of(near_w, b), rows_of(vv, b, 3), preferred_element_type=jnp.float32)
            for b in range(blocks)
        ], axis=0)
        acc[:, cols] = o + jnp.dot(
            glob_e.astype(jnp.bfloat16), vg, preferred_element_type=jnp.float32
        )
        top_s[h] = jnp.broadcast_to(top, top_s.shape[1:])
        sum_s[h] = jnp.broadcast_to(total, sum_s.shape[1:])
        return c

    def finish(h, c):
        cols = pl.ds(pl.multiple_of(h * head_dim, head_dim), head_dim)
        picked = [arr[slot_ref[b * heads + h]] for b in range(blocks)]
        s = jnp.concatenate([
            lax.dot_general(
                q_ref[b * block_len : (b + 1) * block_len, cols], pair[:, 0:head_dim],
                (((1,), (1,)), ((), ())), preferred_element_type=jnp.float32,
            )
            for b, pair in enumerate(picked)
        ], axis=0) * scale
        before = top_s[h]
        top = jnp.maximum(before, jnp.max(s, axis=-1, keepdims=True))
        fade = jnp.exp(before - top)
        expo = jnp.exp(s - top[:, 0:block_len])
        total = sum_s[h] * fade + jnp.sum(expo, axis=-1, keepdims=True)
        weight = expo.astype(jnp.bfloat16)
        o = jnp.concatenate([
            jnp.dot(
                weight[b * block_len : (b + 1) * block_len], pair[:, head_dim:wide],
                preferred_element_type=jnp.float32,
            )
            for b, pair in enumerate(picked)
        ], axis=0)
        att[:, cols] = ((acc[:, cols] * fade + o) * (1.0 / total)).astype(att.dtype)
        return c

    def attend(h0, h1):
        lax.fori_loop(h0, h1, begin, 0)

    each(ship, 1, n // 4)
    advance(1)
    globals_line()
    each(ship, n // 4, n // 2)
    forward(0)
    if lines > 2:
        advance(2)
    globals_plane()
    each(ship, n // 2, n)
    pack(me, arr, me)
    forward(1)
    for t in range(3, lines):
        advance(t)
        if t == 3:
            globals_done()
        forward(t - 1)
    attend(0, heads // 2)
    forward(lines - 1)
    attend(heads // 2, heads)

    each(lambda k: rand(k).wait_recv())
    lax.fori_loop(0, heads, finish, 0)

    for t in range(lines):
        for side in sides(t):
            @pl.when(exists(side, t))
            def _():
                for way in (0, 1):
                    far(side, t, way).wait_recv()
    own_rows.wait()

    kept = out_ref.shape[0]
    depth = full_ref.shape[0] * full_ref.shape[1]
    step = give.shape[2]
    chunks = give.shape[0]

    def product(row, c):
        cols = pl.ds(pl.multiple_of(c * step, step), step)
        return jnp.dot(
            att[pl.ds(pl.multiple_of(row, kept), kept)],
            full_ref[:, :, cols].reshape(depth, step),
            preferred_element_type=jnp.float32,
        )

    def hand(c):
        return pltpu.make_async_remote_copy(
            src_ref=give.at[c], dst_ref=take.at[c], send_sem=core_send.at[c],
            recv_sem=core_recv.at[c], device_id={"head": 1 - hd}, device_id_type=MESH,
        )

    def theirs(c):
        give[c] = product((1 - hd) * kept, c).astype(give.dtype)
        hand(c).start()

    def ours(c):
        mine = product(hd * kept, c).astype(give.dtype).astype(jnp.float32)
        hand(c).wait_recv()
        cols = pl.ds(pl.multiple_of(c * step, step), step)
        out_ref[:, cols] = (mine + take[c].astype(jnp.float32)).astype(out_ref.dtype)

    each(theirs, 0, chunks)
    each(ours, 0, chunks)
    each(lambda c: hand(c).wait_send(), 0, chunks)

    for t in range(lines):
        for side in (0, 1):
            if t < lines - 1:
                @pl.when(passes(side, t))
                def _():
                    along(side, t).wait_send()
        for side in sides(t):
            @pl.when(exists(side, t))
            def _():
                for way in (0, 1):
                    near(side, t, way).wait_send()
                    far(side, t, way).wait_send()
    each(lambda k: code(k).wait_send())
    each(lambda k: rand(k).wait_send())
    for i in range(3):
        plane_cut(i).wait_send()
        plane_give(i).wait_send()
    for dz in range(1, lines):
        line_give(dz).wait_send()
    for copy in edges:
        copy.wait_send()


def layer(glob, places, codes, q, k, v, weight, n, cap, blocks, block_len, head_dim, heads):
    lines = n // 4
    rows, columns = weight.shape
    tokens, width = q.shape
    dma = pltpu.SemaphoreType.DMA
    vmem = pl.BlockSpec(memory_space=pltpu.VMEM)
    smem = pl.BlockSpec(memory_space=pltpu.SMEM)
    hbm = pl.BlockSpec(memory_space=pl.ANY)
    kind = q.dtype
    f32 = jnp.float32
    slots = (n * cap, block_len, 2 * head_dim)
    pair = (block_len, 2 * head_dim)
    chunks = 4
    return pl.pallas_call(
        functools.partial(
            layer_kernel, n, cap, blocks, block_len, head_dim, heads, head_dim ** (-0.5)
        ),
        out_shape=jax.ShapeDtypeStruct((tokens // 2, columns), kind),
        in_specs=[smem, smem, vmem, hbm, hbm, hbm, hbm],
        out_specs=vmem,
        scratch_shapes=[
            pltpu.VMEM(q.shape, kind),
            pltpu.VMEM(q.shape, kind),
            pltpu.VMEM(q.shape, kind),
            pltpu.VMEM((n, rows, columns), kind),
            pltpu.VMEM(q.shape, kind),
            pltpu.VMEM((chunks, tokens // 2, columns // chunks), kind),
            pltpu.VMEM((chunks, tokens // 2, columns // chunks), kind),
            pltpu.VMEM((blocks * heads, block_len, 2 * head_dim), kind),
            pltpu.VMEM(slots, kind),
            pltpu.VMEM(slots, kind),
            pltpu.VMEM(codes.shape, jnp.int32),
            pltpu.SMEM(codes.shape, jnp.int32),
            pltpu.VMEM((2, block_len, width), kind),
            pltpu.VMEM((2, block_len, width), kind),
            pltpu.VMEM((2, heads, *pair), kind),
            pltpu.VMEM((4, heads // 2, *pair), kind),
            pltpu.VMEM((lines, heads // 2, *pair), kind),
            pltpu.VMEM((2, heads, *pair), kind),
            pltpu.VMEM((tokens, width), f32),
            pltpu.VMEM((heads, tokens, LANES), f32),
            pltpu.VMEM((heads, tokens, LANES), f32),
            dma((2, lines)), dma((2, lines)),
            dma((2, lines, 2)), dma((2, lines, 2)),
            dma((2, lines, 2)), dma((2, lines, 2)),
            dma((n,)), dma((n,)), dma((n,)), dma((n,)),
            dma((2, 2)), dma((2, 2)),
            dma((3,)), dma((3,)), dma((lines,)), dma((lines,)), dma((3,)), dma((3,)),
            dma((chunks,)), dma((chunks,)), dma((5,)),
        ],
        compiler_params=pltpu.CompilerParams(
            collective_id=0, has_side_effects=True, vmem_limit_bytes=60 << 20
        ),
        cost_estimate=pl.CostEstimate(
            flops=4 * tokens * 6 * block_len * width,
            transcendentals=tokens * 6 * block_len * heads,
            bytes_accessed=40 * n * rows * columns,
        ),
        name="layer",
    )(glob, places, codes, q, k, v, weight)


def body(queries, keys, values, rand_blocks, global_blocks, out_weight):
    n = lax.axis_size("seq")
    block_count, head_count = rand_blocks.shape
    tokens, width = queries.shape
    block_len = tokens // block_count
    head_dim = width // head_count
    entries = block_count * head_count
    cap = max(2, (2 * entries + n - 1) // n)

    flat_blocks = rand_blocks.reshape(entries)
    owners = flat_blocks // block_count
    head_iota = jnp.arange(entries, dtype=jnp.int32) % head_count
    codes = flat_blocks % block_count * head_count + head_iota
    ranks = ranked(owners)
    target = jnp.arange(n, dtype=jnp.int32)[:, None, None]
    slot = jnp.arange(LANES, dtype=jnp.int32)[None, :, None]
    hits = (owners[None, None, :] == target) & (ranks[None, None, :] == slot)
    outgoing = jnp.sum(jnp.where(hits, codes[None, None, :], 0), axis=2)

    return layer(
        global_blocks, owners * cap + ranks, outgoing.reshape(n, 1, LANES), queries, keys, values,
        out_weight, n, cap, block_count, block_len, head_dim, head_count,
    )


def solution(mesh):
    placed = (
        P("seq", "head"),
        P("seq", "head"),
        P("seq", "head"),
        P("seq", "head"),
        P(),
        P(("head", "seq"), None),
    )
    return jax.shard_map(
        body, mesh=mesh, in_specs=placed, out_specs=P(("seq", "head"), None), check_vma=False
    )
```

```python
import functools

import jax
import jax.numpy as jnp
from jax import lax
from jax.experimental import pallas as pl
from jax.experimental.pallas import tpu as pltpu
from jax.sharding import PartitionSpec as P

MESH = pl.DeviceIdType.MESH
LANES = 128


def layer_kernel(
    n, cap, blocks, block_len, head_dim, heads, scale,
    glob_ref, rand_ref, q_hbm, k_hbm, v_hbm, w_ref,
    out_ref,
    q_ref, k_ref, v_ref, full_ref, att, give, take,
    slot_row, slot_ref, codes_ref, pairs, stage, arr, codes_in, codes, low, high, cand, got_p, got_z, shared,
    acc, top_s, sum_s,
    line_send, line_recv, near_send, near_recv, far_send, far_recv,
    code_send, code_recv, rand_send, rand_recv, edge_send, edge_recv,
    cut_send, cut_recv, line_out, line_in, give_send, give_recv, core_send, core_recv, local,
):
    lines = n // 4
    me = lax.axis_index("seq")
    z, y, x = me // 4, me // 2 % 2, me % 2
    other_y = z * 4 + (1 - y) * 2 + x
    other_x = z * 4 + y * 2 + 1 - x
    half = w_ref.shape[1] // 2
    part = heads // 2
    wide = 2 * head_dim

    hd = lax.axis_index("head")
    loads = [
        pltpu.make_async_copy(src, dst, local.at[2 + i])
        for i, (src, dst) in enumerate(((k_hbm, k_ref), (v_hbm, v_ref), (q_hbm, q_ref)))
    ]
    for copy in loads:
        copy.start()

    barrier = pltpu.get_barrier_semaphore()

    def greet(k, c):
        pl.semaphore_signal(
            barrier, inc=1, device_id={"seq": lax.rem(me + k, n)}, device_id_type=MESH
        )
        return c

    lax.fori_loop(1, n, greet, 0)
    pl.semaphore_signal(barrier, inc=1, device_id={"head": 1 - hd}, device_id_type=MESH)

    def named(e):
        return rand_ref[lax.div(e, heads), lax.rem(e, heads)]

    owner_of = lax.broadcasted_iota(jnp.int32, (n, LANES), 0)
    slot_of = lax.broadcasted_iota(jnp.int32, (n, LANES), 1)

    def enlist(e, c):
        seen, table, places = c
        block = named(e)
        asked = owner_of == lax.div(block, blocks)
        entry = lax.rem(block, blocks) * heads + lax.rem(e, heads)
        table = jnp.where(asked & (slot_of == seen), entry, table)
        places = jnp.where(asked & (slot_of == e), owner_of * cap + seen, places)
        return jnp.where(asked, seen + 1, seen), table, places

    zeros = jnp.zeros((n, LANES), jnp.int32)
    _, table, places = lax.fori_loop(0, blocks * heads, enlist, (zeros, zeros, zeros))
    slot_row[...] = jnp.sum(places, axis=0, keepdims=True)
    slots_down = pltpu.make_async_copy(slot_row, slot_ref, local.at[5])
    slots_down.start()
    for t in range(n):
        codes_ref[t] = table[t : t + 1]
    pl.semaphore_wait(barrier, n)

    def remote(src, dst, send, recv, target):
        return pltpu.make_async_remote_copy(
            src_ref=src, dst_ref=dst, send_sem=send, recv_sem=recv,
            device_id={"seq": target}, device_id_type=MESH,
        )

    def origin(side, t):
        return (z - t if side == 0 else z + t) * 4

    def exists(side, t):
        return z - t >= 0 if side == 0 else z + t < lines

    def held(side, t):
        return w_ref if t == 0 else full_ref.at[origin(side, t) + y * 2 + x]

    def along(side, t):
        target = me + 4 if side == 0 else me - 4
        index = origin(side, t) + y * 2 + x
        return remote(
            held(side, t), full_ref.at[index], line_send.at[side, t], line_recv.at[side, t], target
        )

    def passes(side, t):
        ahead = z + 1 < lines if side == 0 else z >= 1
        return jnp.logical_and(exists(side, t), ahead)

    def near(side, t, way):
        index = origin(side, t) + y * 2 + x
        return remote(
            held(side, t), full_ref.at[index], near_send.at[side, t, way],
            near_recv.at[side, t, way], other_y if way == 0 else other_x,
        )

    def far(side, t, way):
        index = origin(side, t) + (
            (1 - y) * 2 + x if way == 0 else y * 2 + 1 - x
        )
        cols = pl.ds(way * half, half)
        return remote(
            full_ref.at[index, :, cols], full_ref.at[index, :, cols], far_send.at[side, t, way],
            far_recv.at[side, t, way], other_x if way == 0 else other_y,
        )

    def sides(t):
        return (0,) if t == 0 else (0, 1)

    def advance(t):
        for side in (0, 1):
            if t > 0:
                @pl.when(exists(side, t))
                def _():
                    along(side, t - 1).wait_recv()
            if t < lines - 1:
                @pl.when(passes(side, t))
                def _():
                    along(side, t).start()
        for side in sides(t):
            @pl.when(exists(side, t))
            def _():
                near(side, t, 0).start()
                near(side, t, 1).start()

    def forward(t):
        for side in sides(t):
            @pl.when(exists(side, t))
            def _():
                for way in (0, 1):
                    near(side, t, way).wait_recv()
                    far(side, t, way).start()

    def code(k):
        target = lax.rem(me + k, n)
        return remote(
            codes_ref.at[target], codes_in.at[me], code_send.at[k], code_recv.at[k], target
        )

    def stride(k):
        return lax.rem(me + lax.rem(k * (n // 2 - 1), n), n)

    def rand(k):
        target = stride(k)
        return remote(
            stage.at[pl.ds(target * cap, cap)], arr.at[pl.ds(me * cap, cap)],
            rand_send.at[k], rand_recv.at[k], target,
        )

    def each(body, first=1, last=n):
        def step(k, c):
            body(k)
            return c
        lax.fori_loop(first, last, step, 0)

    each(lambda k: code(k).start())
    codes_in[pl.ds(me, 1)] = codes_ref[pl.ds(me, 1)]

    own_rows = pltpu.make_async_copy(w_ref, full_ref.at[me], local.at[0])
    own_rows.start()
    advance(0)

    tail = (blocks - 1) * block_len
    up, down = lax.rem(me + 1, n), lax.rem(me + n - 1, n)
    edges = []
    for i, ref in enumerate((k_hbm, v_hbm)):
        edges.append(remote(
            ref.at[tail : tail + block_len], low.at[i], edge_send.at[0, i], edge_recv.at[0, i], up
        ))
        edges.append(remote(
            ref.at[0:block_len], high.at[i], edge_send.at[1, i], edge_recv.at[1, i], down
        ))
    for copy in edges:
        copy.start()

    for copy in loads:
        copy.wait()
    for b in range(blocks):
        rows = slice(b * block_len, (b + 1) * block_len)
        for h in range(heads):
            cols = slice(h * head_dim, (h + 1) * head_dim)
            pairs[b * heads + h, :, 0:head_dim] = k_ref[rows, cols]
            pairs[b * heads + h, :, head_dim:wide] = v_ref[rows, cols]

    plane = 2 * y + x
    mates = ((0, 1), (1, 0), (1, 1))

    def mate(dy, dx):
        return lax.rem(y + dy, 2), lax.rem(x + dx, 2)

    def plane_cut(i):
        ty, tx = mate(*mates[i])
        return remote(
            cand.at[tx, pl.ds(ty * part, part)], got_p.at[plane], cut_send.at[i], cut_recv.at[i],
            z * 4 + ty * 2 + tx,
        )

    def line_give(dz):
        to = lax.rem(z + dz, lines)
        return remote(got_z.at[z], got_z.at[z], line_out.at[dz], line_in.at[dz], to * 4 + plane)

    def plane_give(i):
        ty, tx = mate(*mates[i])
        piece = shared.at[x, pl.ds(y * part, part)]
        return remote(piece, piece, give_send.at[i], give_recv.at[i], z * 4 + ty * 2 + tx)

    for g in range(2):
        base = glob_ref[g] % blocks * heads
        for h in range(heads):
            cand[g, h] = pairs[base + h]
    for i in range(3):
        plane_cut(i).start()
    got_p[plane] = cand[x, pl.ds(y * part, part)]
    holder = glob_ref[x] // blocks

    def globals_line():
        for i in range(3):
            plane_cut(i).wait_recv()
        got_z[z] = got_p[holder % 4]
        for dz in range(1, lines):
            line_give(dz).start()

    def globals_plane():
        for dz in range(1, lines):
            line_give(dz).wait_recv()
        shared[x, pl.ds(y * part, part)] = got_z[holder // 4]
        for i in range(3):
            plane_give(i).start()

    def globals_done():
        for i in range(3):
            plane_give(i).wait_recv()
        for copy in edges:
            copy.wait_recv()

    each(lambda k: code(k).wait_recv())
    to_smem = pltpu.make_async_copy(codes_in, codes, local.at[1])
    to_smem.start()
    to_smem.wait()

    def pack(target, out, place):
        for s in range(cap):
            out[place * cap + s] = pairs[codes[target, 0, s]]

    def ship(k):
        target = stride(k)
        pack(target, stage, target)
        rand(k).start()

    def begin(h, c):
        cols = pl.ds(pl.multiple_of(h * head_dim, head_dim), head_dim)
        kk = jnp.concatenate([low[0, :, cols], k_ref[:, cols], high[0, :, cols]], axis=0)
        vv = jnp.concatenate([low[1, :, cols], v_ref[:, cols], high[1, :, cols]], axis=0)
        kg = [shared[i, h, :, 0:head_dim] for i in range(2)]
        vg = [shared[i, h, :, head_dim:wide] for i in range(2)]
        kg, vg = jnp.concatenate(kg, axis=0), jnp.concatenate(vg, axis=0)
        q = q_ref[:, cols]

        def against(rows, table):
            return lax.dot_general(
                rows, table, (((1,), (1,)), ((), ())), preferred_element_type=jnp.float32
            )

        def rows_of(array, b, count=1):
            return array[b * block_len : (b + count) * block_len]

        near_s = jnp.concatenate(
            [against(rows_of(q, b), rows_of(kk, b, 3)) for b in range(blocks)], axis=0
        ) * scale
        glob_s = against(q, kg) * scale
        top = jnp.maximum(
            jnp.max(near_s, axis=-1, keepdims=True), jnp.max(glob_s, axis=-1, keepdims=True)
        )
        near_e, glob_e = jnp.exp(near_s - top), jnp.exp(glob_s - top)
        total = jnp.sum(near_e, axis=-1, keepdims=True) + jnp.sum(glob_e, axis=-1, keepdims=True)
        near_w = near_e.astype(jnp.bfloat16)
        o = jnp.concatenate([
            jnp.dot(rows_of(near_w, b), rows_of(vv, b, 3), preferred_element_type=jnp.float32)
            for b in range(blocks)
        ], axis=0)
        acc[:, cols] = o + jnp.dot(
            glob_e.astype(jnp.bfloat16), vg, preferred_element_type=jnp.float32
        )
        top_s[h] = jnp.broadcast_to(top, top_s.shape[1:])
        sum_s[h] = jnp.broadcast_to(total, sum_s.shape[1:])
        return c

    def finish(h, c):
        cols = pl.ds(pl.multiple_of(h * head_dim, head_dim), head_dim)
        picked = [arr[slot_ref[0, b * heads + h]] for b in range(blocks)]
        s = jnp.concatenate([
            lax.dot_general(
                q_ref[b * block_len : (b + 1) * block_len, cols], pair[:, 0:head_dim],
                (((1,), (1,)), ((), ())), preferred_element_type=jnp.float32,
            )
            for b, pair in enumerate(picked)
        ], axis=0) * scale
        before = top_s[h]
        top = jnp.maximum(before, jnp.max(s, axis=-1, keepdims=True))
        fade = jnp.exp(before - top)
        expo = jnp.exp(s - top[:, 0:block_len])
        total = sum_s[h] * fade + jnp.sum(expo, axis=-1, keepdims=True)
        weight = expo.astype(jnp.bfloat16)
        o = jnp.concatenate([
            jnp.dot(
                weight[b * block_len : (b + 1) * block_len], pair[:, head_dim:wide],
                preferred_element_type=jnp.float32,
            )
            for b, pair in enumerate(picked)
        ], axis=0)
        att[:, cols] = ((acc[:, cols] * fade + o) * (1.0 / total)).astype(att.dtype)
        return c

    def attend(h0, h1):
        lax.fori_loop(h0, h1, begin, 0)

    each(ship, 1, n // 4)
    advance(1)
    globals_line()
    each(ship, n // 4, n // 2)
    forward(0)
    if lines > 2:
        advance(2)
    globals_plane()
    each(ship, n // 2, n)
    pack(me, arr, me)
    forward(1)
    for t in range(3, lines):
        advance(t)
        if t == 3:
            globals_done()
        forward(t - 1)
    attend(0, heads // 2)
    forward(lines - 1)
    attend(heads // 2, heads)
    slots_down.wait()

    each(lambda k: rand(k).wait_recv())
    lax.fori_loop(0, heads, finish, 0)

    for t in range(lines):
        for side in sides(t):
            @pl.when(exists(side, t))
            def _():
                for way in (0, 1):
                    far(side, t, way).wait_recv()
    own_rows.wait()

    kept = out_ref.shape[0]
    depth = full_ref.shape[0] * full_ref.shape[1]
    step = give.shape[2]
    chunks = give.shape[0]

    def product(row, c):
        cols = pl.ds(pl.multiple_of(c * step, step), step)
        return jnp.dot(
            att[pl.ds(pl.multiple_of(row, kept), kept)],
            full_ref[:, :, cols].reshape(depth, step),
            preferred_element_type=jnp.float32,
        )

    def hand(c):
        return pltpu.make_async_remote_copy(
            src_ref=give.at[c], dst_ref=take.at[c], send_sem=core_send.at[c],
            recv_sem=core_recv.at[c], device_id={"head": 1 - hd}, device_id_type=MESH,
        )

    def theirs(c):
        give[c] = product((1 - hd) * kept, c).astype(give.dtype)
        hand(c).start()

    def ours(c):
        mine = product(hd * kept, c).astype(give.dtype).astype(jnp.float32)
        hand(c).wait_recv()
        cols = pl.ds(pl.multiple_of(c * step, step), step)
        out_ref[:, cols] = (mine + take[c].astype(jnp.float32)).astype(out_ref.dtype)

    each(theirs, 0, chunks)
    each(ours, 0, chunks)
    each(lambda c: hand(c).wait_send(), 0, chunks)

    for t in range(lines):
        for side in (0, 1):
            if t < lines - 1:
                @pl.when(passes(side, t))
                def _():
                    along(side, t).wait_send()
        for side in sides(t):
            @pl.when(exists(side, t))
            def _():
                for way in (0, 1):
                    near(side, t, way).wait_send()
                    far(side, t, way).wait_send()
    each(lambda k: code(k).wait_send())
    each(lambda k: rand(k).wait_send())
    for i in range(3):
        plane_cut(i).wait_send()
        plane_give(i).wait_send()
    for dz in range(1, lines):
        line_give(dz).wait_send()
    for copy in edges:
        copy.wait_send()


def layer(glob, rand, q, k, v, weight, n, cap, blocks, block_len, head_dim, heads):
    lines = n // 4
    codes = (n, 1, LANES)
    rows, columns = weight.shape
    tokens, width = q.shape
    dma = pltpu.SemaphoreType.DMA
    vmem = pl.BlockSpec(memory_space=pltpu.VMEM)
    smem = pl.BlockSpec(memory_space=pltpu.SMEM)
    hbm = pl.BlockSpec(memory_space=pl.ANY)
    kind = q.dtype
    f32 = jnp.float32
    slots = (n * cap, block_len, 2 * head_dim)
    pair = (block_len, 2 * head_dim)
    chunks = 4
    return pl.pallas_call(
        functools.partial(
            layer_kernel, n, cap, blocks, block_len, head_dim, heads, head_dim ** (-0.5)
        ),
        out_shape=jax.ShapeDtypeStruct((tokens // 2, columns), kind),
        in_specs=[smem, smem, hbm, hbm, hbm, hbm],
        out_specs=vmem,
        scratch_shapes=[
            pltpu.VMEM(q.shape, kind),
            pltpu.VMEM(q.shape, kind),
            pltpu.VMEM(q.shape, kind),
            pltpu.VMEM((n, rows, columns), kind),
            pltpu.VMEM(q.shape, kind),
            pltpu.VMEM((chunks, tokens // 2, columns // chunks), kind),
            pltpu.VMEM((chunks, tokens // 2, columns // chunks), kind),
            pltpu.VMEM((1, LANES), jnp.int32),
            pltpu.SMEM((1, LANES), jnp.int32),
            pltpu.VMEM(codes, jnp.int32),
            pltpu.VMEM((blocks * heads, block_len, 2 * head_dim), kind),
            pltpu.VMEM(slots, kind),
            pltpu.VMEM(slots, kind),
            pltpu.VMEM(codes, jnp.int32),
            pltpu.SMEM(codes, jnp.int32),
            pltpu.VMEM((2, block_len, width), kind),
            pltpu.VMEM((2, block_len, width), kind),
            pltpu.VMEM((2, heads, *pair), kind),
            pltpu.VMEM((4, heads // 2, *pair), kind),
            pltpu.VMEM((lines, heads // 2, *pair), kind),
            pltpu.VMEM((2, heads, *pair), kind),
            pltpu.VMEM((tokens, width), f32),
            pltpu.VMEM((heads, tokens, LANES), f32),
            pltpu.VMEM((heads, tokens, LANES), f32),
            dma((2, lines)), dma((2, lines)),
            dma((2, lines, 2)), dma((2, lines, 2)),
            dma((2, lines, 2)), dma((2, lines, 2)),
            dma((n,)), dma((n,)), dma((n,)), dma((n,)),
            dma((2, 2)), dma((2, 2)),
            dma((3,)), dma((3,)), dma((lines,)), dma((lines,)), dma((3,)), dma((3,)),
            dma((chunks,)), dma((chunks,)), dma((6,)),
        ],
        compiler_params=pltpu.CompilerParams(
            collective_id=0, has_side_effects=True, vmem_limit_bytes=60 << 20
        ),
        cost_estimate=pl.CostEstimate(
            flops=4 * tokens * 6 * block_len * width,
            transcendentals=tokens * 6 * block_len * heads,
            bytes_accessed=40 * n * rows * columns,
        ),
        name="layer",
    )(glob, rand, q, k, v, weight)


def body(queries, keys, values, rand_blocks, global_blocks, out_weight):
    n = lax.axis_size("seq")
    block_count, head_count = rand_blocks.shape
    tokens, width = queries.shape
    block_len = tokens // block_count
    head_dim = width // head_count
    entries = block_count * head_count
    cap = max(2, (2 * entries + n - 1) // n)

    return layer(
        global_blocks, rand_blocks, queries, keys, values, out_weight,
        n, cap, block_count, block_len, head_dim, head_count,
    )


def solution(mesh):
    placed = (
        P("seq", "head"),
        P("seq", "head"),
        P("seq", "head"),
        P("seq", "head"),
        P(),
        P(("head", "seq"), None),
    )
    return jax.shard_map(
        body, mesh=mesh, in_specs=placed, out_specs=P(("seq", "head"), None), check_vma=False
    )
```

```python
import functools

import jax
import jax.numpy as jnp
from jax import lax
from jax.experimental import pallas as pl
from jax.experimental.pallas import tpu as pltpu
from jax.sharding import PartitionSpec as P

MESH = pl.DeviceIdType.MESH
LANES = 128


def layer_kernel(
    n, cap, blocks, block_len, head_dim, heads, scale,
    glob_ref, rand_ref, q_hbm, k_hbm, v_hbm, w_ref,
    out_ref,
    q_ref, k_ref, v_ref, full_ref, att, give, take,
    slot_row, slot_ref, codes_ref, pairs, stage, arr, codes_in, codes, low, high, cand, got_p, got_z, shared,
    acc, top_s, sum_s,
    line_send, line_recv, near_send, near_recv, far_send, far_recv,
    code_send, code_recv, rand_send, rand_recv, edge_send, edge_recv,
    cut_send, cut_recv, line_out, line_in, give_send, give_recv, core_send, core_recv, local,
):
    lines = n // 4
    me = lax.axis_index("seq")
    z, y, x = me // 4, me // 2 % 2, me % 2
    other_y = z * 4 + (1 - y) * 2 + x
    other_x = z * 4 + y * 2 + 1 - x
    half = w_ref.shape[1] // 2
    part = heads // 2
    wide = 2 * head_dim

    hd = lax.axis_index("head")
    loads = [
        pltpu.make_async_copy(src, dst, local.at[2 + i])
        for i, (src, dst) in enumerate(((k_hbm, k_ref), (v_hbm, v_ref), (q_hbm, q_ref)))
    ]
    for copy in loads:
        copy.start()

    barrier = pltpu.get_barrier_semaphore()

    def greet(k, c):
        pl.semaphore_signal(
            barrier, inc=1, device_id={"seq": lax.rem(me + k, n)}, device_id_type=MESH
        )
        return c

    lax.fori_loop(1, n, greet, 0)
    pl.semaphore_signal(barrier, inc=1, device_id={"head": 1 - hd}, device_id_type=MESH)

    def named(e):
        return rand_ref[lax.div(e, heads), lax.rem(e, heads)]

    owner_of = lax.broadcasted_iota(jnp.int32, (n, LANES), 0)
    slot_of = lax.broadcasted_iota(jnp.int32, (n, LANES), 1)

    def enlist(e, c):
        seen, table, places = c
        block = named(e)
        asked = owner_of == lax.div(block, blocks)
        entry = lax.rem(block, blocks) * heads + lax.rem(e, heads)
        table = jnp.where(asked & (slot_of == seen), entry, table)
        places = jnp.where(asked & (slot_of == e), owner_of * cap + seen, places)
        return jnp.where(asked, seen + 1, seen), table, places

    zeros = jnp.zeros((n, LANES), jnp.int32)
    _, table, places = lax.fori_loop(0, blocks * heads, enlist, (zeros, zeros, zeros))
    slot_row[...] = jnp.sum(places, axis=0, keepdims=True)
    slots_down = pltpu.make_async_copy(slot_row, slot_ref, local.at[5])
    slots_down.start()
    for t in range(n):
        codes_ref[t] = table[t : t + 1]
    pl.semaphore_wait(barrier, n)

    def remote(src, dst, send, recv, target):
        return pltpu.make_async_remote_copy(
            src_ref=src, dst_ref=dst, send_sem=send, recv_sem=recv,
            device_id={"seq": target}, device_id_type=MESH,
        )

    def origin(side, t):
        return (z - t if side == 0 else z + t) * 4

    def exists(side, t):
        return z - t >= 0 if side == 0 else z + t < lines

    def held(side, t):
        return w_ref if t == 0 else full_ref.at[origin(side, t) + y * 2 + x]

    def along(side, t):
        target = me + 4 if side == 0 else me - 4
        index = origin(side, t) + y * 2 + x
        return remote(
            held(side, t), full_ref.at[index], line_send.at[side, t], line_recv.at[side, t], target
        )

    def passes(side, t):
        ahead = z + 1 < lines if side == 0 else z >= 1
        return jnp.logical_and(exists(side, t), ahead)

    def near(side, t, way):
        index = origin(side, t) + y * 2 + x
        return remote(
            held(side, t), full_ref.at[index], near_send.at[side, t, way],
            near_recv.at[side, t, way], other_y if way == 0 else other_x,
        )

    def far(side, t, way):
        index = origin(side, t) + (
            (1 - y) * 2 + x if way == 0 else y * 2 + 1 - x
        )
        cols = pl.ds(way * half, half)
        return remote(
            full_ref.at[index, :, cols], full_ref.at[index, :, cols], far_send.at[side, t, way],
            far_recv.at[side, t, way], other_x if way == 0 else other_y,
        )

    def sides(t):
        return (0,) if t == 0 else (0, 1)

    def advance(t):
        for side in (0, 1):
            if t > 0:
                @pl.when(exists(side, t))
                def _():
                    along(side, t - 1).wait_recv()
            if t < lines - 1:
                @pl.when(passes(side, t))
                def _():
                    along(side, t).start()
        for side in sides(t):
            @pl.when(exists(side, t))
            def _():
                near(side, t, 0).start()
                near(side, t, 1).start()

    def forward(t):
        for side in sides(t):
            @pl.when(exists(side, t))
            def _():
                for way in (0, 1):
                    near(side, t, way).wait_recv()
                    far(side, t, way).start()

    def code(k):
        target = lax.rem(me + k, n)
        return remote(
            codes_ref.at[target], codes_in.at[me], code_send.at[k], code_recv.at[k], target
        )

    def stride(k):
        return lax.rem(me + lax.rem(k * 5, n), n)

    def rand(k):
        target = stride(k)
        return remote(
            stage.at[pl.ds(target * cap, cap)], arr.at[pl.ds(me * cap, cap)],
            rand_send.at[k], rand_recv.at[k], target,
        )

    def each(body, first=1, last=n):
        def step(k, c):
            body(k)
            return c
        lax.fori_loop(first, last, step, 0)

    each(lambda k: code(k).start())
    codes_in[pl.ds(me, 1)] = codes_ref[pl.ds(me, 1)]

    own_rows = pltpu.make_async_copy(w_ref, full_ref.at[me], local.at[0])
    own_rows.start()
    advance(0)

    tail = (blocks - 1) * block_len
    up, down = lax.rem(me + 1, n), lax.rem(me + n - 1, n)
    edges = []
    for i, ref in enumerate((k_hbm, v_hbm)):
        edges.append(remote(
            ref.at[tail : tail + block_len], low.at[i], edge_send.at[0, i], edge_recv.at[0, i], up
        ))
        edges.append(remote(
            ref.at[0:block_len], high.at[i], edge_send.at[1, i], edge_recv.at[1, i], down
        ))
    for copy in edges:
        copy.start()

    for copy in loads:
        copy.wait()
    for b in range(blocks):
        rows = slice(b * block_len, (b + 1) * block_len)
        for h in range(heads):
            cols = slice(h * head_dim, (h + 1) * head_dim)
            pairs[b * heads + h, :, 0:head_dim] = k_ref[rows, cols]
            pairs[b * heads + h, :, head_dim:wide] = v_ref[rows, cols]

    plane = 2 * y + x
    mates = ((0, 1), (1, 0), (1, 1))

    def mate(dy, dx):
        return lax.rem(y + dy, 2), lax.rem(x + dx, 2)

    def plane_cut(i):
        ty, tx = mate(*mates[i])
        return remote(
            cand.at[tx, pl.ds(ty * part, part)], got_p.at[plane], cut_send.at[i], cut_recv.at[i],
            z * 4 + ty * 2 + tx,
        )

    def line_give(dz):
        to = lax.rem(z + dz, lines)
        return remote(got_z.at[z], got_z.at[z], line_out.at[dz], line_in.at[dz], to * 4 + plane)

    def plane_give(i):
        ty, tx = mate(*mates[i])
        piece = shared.at[x, pl.ds(y * part, part)]
        return remote(piece, piece, give_send.at[i], give_recv.at[i], z * 4 + ty * 2 + tx)

    for g in range(2):
        base = glob_ref[g] % blocks * heads
        for h in range(heads):
            cand[g, h] = pairs[base + h]
    for i in range(3):
        plane_cut(i).start()
    got_p[plane] = cand[x, pl.ds(y * part, part)]
    holder = glob_ref[x] // blocks

    def globals_line():
        for i in range(3):
            plane_cut(i).wait_recv()
        got_z[z] = got_p[holder % 4]
        for dz in range(1, lines):
            line_give(dz).start()

    def globals_plane():
        for dz in range(1, lines):
            line_give(dz).wait_recv()
        shared[x, pl.ds(y * part, part)] = got_z[holder // 4]
        for i in range(3):
            plane_give(i).start()

    def globals_done():
        for i in range(3):
            plane_give(i).wait_recv()
        for copy in edges:
            copy.wait_recv()

    each(lambda k: code(k).wait_recv())
    to_smem = pltpu.make_async_copy(codes_in, codes, local.at[1])
    to_smem.start()
    to_smem.wait()

    def pack(target, out, place):
        for s in range(cap):
            out[place * cap + s] = pairs[codes[target, 0, s]]

    def ship(k):
        target = stride(k)
        pack(target, stage, target)
        rand(k).start()

    def begin(h, c):
        cols = pl.ds(pl.multiple_of(h * head_dim, head_dim), head_dim)
        kk = jnp.concatenate([low[0, :, cols], k_ref[:, cols], high[0, :, cols]], axis=0)
        vv = jnp.concatenate([low[1, :, cols], v_ref[:, cols], high[1, :, cols]], axis=0)
        kg = [shared[i, h, :, 0:head_dim] for i in range(2)]
        vg = [shared[i, h, :, head_dim:wide] for i in range(2)]
        kg, vg = jnp.concatenate(kg, axis=0), jnp.concatenate(vg, axis=0)
        q = q_ref[:, cols]

        def against(rows, table):
            return lax.dot_general(
                rows, table, (((1,), (1,)), ((), ())), preferred_element_type=jnp.float32
            )

        def rows_of(array, b, count=1):
            return array[b * block_len : (b + count) * block_len]

        near_s = jnp.concatenate(
            [against(rows_of(q, b), rows_of(kk, b, 3)) for b in range(blocks)], axis=0
        ) * scale
        glob_s = against(q, kg) * scale
        top = jnp.maximum(
            jnp.max(near_s, axis=-1, keepdims=True), jnp.max(glob_s, axis=-1, keepdims=True)
        )
        near_e, glob_e = jnp.exp(near_s - top), jnp.exp(glob_s - top)
        total = jnp.sum(near_e, axis=-1, keepdims=True) + jnp.sum(glob_e, axis=-1, keepdims=True)
        near_w = near_e.astype(jnp.bfloat16)
        o = jnp.concatenate([
            jnp.dot(rows_of(near_w, b), rows_of(vv, b, 3), preferred_element_type=jnp.float32)
            for b in range(blocks)
        ], axis=0)
        acc[:, cols] = o + jnp.dot(
            glob_e.astype(jnp.bfloat16), vg, preferred_element_type=jnp.float32
        )
        top_s[h] = jnp.broadcast_to(top, top_s.shape[1:])
        sum_s[h] = jnp.broadcast_to(total, sum_s.shape[1:])
        return c

    def finish(h, c):
        cols = pl.ds(pl.multiple_of(h * head_dim, head_dim), head_dim)
        picked = [arr[slot_ref[0, b * heads + h]] for b in range(blocks)]
        s = jnp.concatenate([
            lax.dot_general(
                q_ref[b * block_len : (b + 1) * block_len, cols], pair[:, 0:head_dim],
                (((1,), (1,)), ((), ())), preferred_element_type=jnp.float32,
            )
            for b, pair in enumerate(picked)
        ], axis=0) * scale
        before = top_s[h]
        top = jnp.maximum(before, jnp.max(s, axis=-1, keepdims=True))
        fade = jnp.exp(before - top)
        expo = jnp.exp(s - top[:, 0:block_len])
        total = sum_s[h] * fade + jnp.sum(expo, axis=-1, keepdims=True)
        weight = expo.astype(jnp.bfloat16)
        o = jnp.concatenate([
            jnp.dot(
                weight[b * block_len : (b + 1) * block_len], pair[:, head_dim:wide],
                preferred_element_type=jnp.float32,
            )
            for b, pair in enumerate(picked)
        ], axis=0)
        att[:, cols] = ((acc[:, cols] * fade + o) * (1.0 / total)).astype(att.dtype)
        return c

    def attend(h0, h1):
        lax.fori_loop(h0, h1, begin, 0)

    each(ship, 1, n // 4)
    advance(1)
    globals_line()
    each(ship, n // 4, n // 2)
    forward(0)
    if lines > 2:
        advance(2)
    globals_plane()
    each(ship, n // 2, n)
    pack(me, arr, me)
    forward(1)
    for t in range(3, lines):
        advance(t)
        if t == 3:
            globals_done()
        forward(t - 1)
    attend(0, heads // 2)
    forward(lines - 1)
    attend(heads // 2, heads)
    slots_down.wait()

    each(lambda k: rand(k).wait_recv())
    lax.fori_loop(0, heads, finish, 0)

    for t in range(lines):
        for side in sides(t):
            @pl.when(exists(side, t))
            def _():
                for way in (0, 1):
                    far(side, t, way).wait_recv()
    own_rows.wait()

    kept = out_ref.shape[0]
    depth = full_ref.shape[0] * full_ref.shape[1]
    step = give.shape[2]
    chunks = give.shape[0]

    def product(row, c):
        cols = pl.ds(pl.multiple_of(c * step, step), step)
        return jnp.dot(
            att[pl.ds(pl.multiple_of(row, kept), kept)],
            full_ref[:, :, cols].reshape(depth, step),
            preferred_element_type=jnp.float32,
        )

    def hand(c):
        return pltpu.make_async_remote_copy(
            src_ref=give.at[c], dst_ref=take.at[c], send_sem=core_send.at[c],
            recv_sem=core_recv.at[c], device_id={"head": 1 - hd}, device_id_type=MESH,
        )

    def theirs(c):
        give[c] = product((1 - hd) * kept, c).astype(give.dtype)
        hand(c).start()

    def ours(c):
        mine = product(hd * kept, c).astype(give.dtype).astype(jnp.float32)
        hand(c).wait_recv()
        cols = pl.ds(pl.multiple_of(c * step, step), step)
        out_ref[:, cols] = (mine + take[c].astype(jnp.float32)).astype(out_ref.dtype)

    each(theirs, 0, chunks)
    each(ours, 0, chunks)
    each(lambda c: hand(c).wait_send(), 0, chunks)

    for t in range(lines):
        for side in (0, 1):
            if t < lines - 1:
                @pl.when(passes(side, t))
                def _():
                    along(side, t).wait_send()
        for side in sides(t):
            @pl.when(exists(side, t))
            def _():
                for way in (0, 1):
                    near(side, t, way).wait_send()
                    far(side, t, way).wait_send()
    each(lambda k: code(k).wait_send())
    each(lambda k: rand(k).wait_send())
    for i in range(3):
        plane_cut(i).wait_send()
        plane_give(i).wait_send()
    for dz in range(1, lines):
        line_give(dz).wait_send()
    for copy in edges:
        copy.wait_send()


def layer(glob, rand, q, k, v, weight, n, cap, blocks, block_len, head_dim, heads):
    lines = n // 4
    codes = (n, 1, LANES)
    rows, columns = weight.shape
    tokens, width = q.shape
    dma = pltpu.SemaphoreType.DMA
    vmem = pl.BlockSpec(memory_space=pltpu.VMEM)
    smem = pl.BlockSpec(memory_space=pltpu.SMEM)
    hbm = pl.BlockSpec(memory_space=pl.ANY)
    kind = q.dtype
    f32 = jnp.float32
    slots = (n * cap, block_len, 2 * head_dim)
    pair = (block_len, 2 * head_dim)
    chunks = 4
    return pl.pallas_call(
        functools.partial(
            layer_kernel, n, cap, blocks, block_len, head_dim, heads, head_dim ** (-0.5)
        ),
        out_shape=jax.ShapeDtypeStruct((tokens // 2, columns), kind),
        in_specs=[smem, smem, hbm, hbm, hbm, hbm],
        out_specs=vmem,
        scratch_shapes=[
            pltpu.VMEM(q.shape, kind),
            pltpu.VMEM(q.shape, kind),
            pltpu.VMEM(q.shape, kind),
            pltpu.VMEM((n, rows, columns), kind),
            pltpu.VMEM(q.shape, kind),
            pltpu.VMEM((chunks, tokens // 2, columns // chunks), kind),
            pltpu.VMEM((chunks, tokens // 2, columns // chunks), kind),
            pltpu.VMEM((1, LANES), jnp.int32),
            pltpu.SMEM((1, LANES), jnp.int32),
            pltpu.VMEM(codes, jnp.int32),
            pltpu.VMEM((blocks * heads, block_len, 2 * head_dim), kind),
            pltpu.VMEM(slots, kind),
            pltpu.VMEM(slots, kind),
            pltpu.VMEM(codes, jnp.int32),
            pltpu.SMEM(codes, jnp.int32),
            pltpu.VMEM((2, block_len, width), kind),
            pltpu.VMEM((2, block_len, width), kind),
            pltpu.VMEM((2, heads, *pair), kind),
            pltpu.VMEM((4, heads // 2, *pair), kind),
            pltpu.VMEM((lines, heads // 2, *pair), kind),
            pltpu.VMEM((2, heads, *pair), kind),
            pltpu.VMEM((tokens, width), f32),
            pltpu.VMEM((heads, tokens, LANES), f32),
            pltpu.VMEM((heads, tokens, LANES), f32),
            dma((2, lines)), dma((2, lines)),
            dma((2, lines, 2)), dma((2, lines, 2)),
            dma((2, lines, 2)), dma((2, lines, 2)),
            dma((n,)), dma((n,)), dma((n,)), dma((n,)),
            dma((2, 2)), dma((2, 2)),
            dma((3,)), dma((3,)), dma((lines,)), dma((lines,)), dma((3,)), dma((3,)),
            dma((chunks,)), dma((chunks,)), dma((6,)),
        ],
        compiler_params=pltpu.CompilerParams(
            collective_id=0, has_side_effects=True, vmem_limit_bytes=60 << 20
        ),
        cost_estimate=pl.CostEstimate(
            flops=4 * tokens * 6 * block_len * width,
            transcendentals=tokens * 6 * block_len * heads,
            bytes_accessed=40 * n * rows * columns,
        ),
        name="layer",
    )(glob, rand, q, k, v, weight)


def body(queries, keys, values, rand_blocks, global_blocks, out_weight):
    n = lax.axis_size("seq")
    block_count, head_count = rand_blocks.shape
    tokens, width = queries.shape
    block_len = tokens // block_count
    head_dim = width // head_count
    entries = block_count * head_count
    cap = max(2, (2 * entries + n - 1) // n)

    return layer(
        global_blocks, rand_blocks, queries, keys, values, out_weight,
        n, cap, block_count, block_len, head_dim, head_count,
    )


def solution(mesh):
    placed = (
        P("seq", "head"),
        P("seq", "head"),
        P("seq", "head"),
        P("seq", "head"),
        P(),
        P(("head", "seq"), None),
    )
    return jax.shard_map(
        body, mesh=mesh, in_specs=placed, out_specs=P(("seq", "head"), None), check_vma=False
    )
```
